1024 devices in a mesh: ctx: 64 (over x, z_lo, core), tp: 16 (over y, z_hi).
Axes of the slice: x: 4, y: 8, z: 16 (z_hi: 2, z_lo: 8; z = z_hi * 8 + z_lo), core: 2. Of those that a mesh axis runs over, the one named last changes fastest.
Arguments:
- query_in: bfloat16 [8192, 4096], P('ctx', 'tp'), may hold values from -6 to 6
- key_in: bfloat16 [8192, 4096], P('ctx', 'tp'), may hold values from -6 to 6
- value_in: bfloat16 [8192, 4096], P('ctx', 'tp'), may hold values from -6 to 6
- long_filter: bfloat16 [8192, 4096], P('ctx', 'tp'), may hold values from -1.1 to 1.1
- short_taps: bfloat16 [3, 3, 4096], P(None, None, 'tp'), may hold values from -3.5 to 3.5
- out_grad: bfloat16 [8192, 4096], P('ctx', 'tp'), may hold values from -6 to 6
Outputs:
- output: bfloat16 [8192, 4096], P('ctx', 'tp')
- query_grad: bfloat16 [8192, 4096], P('ctx', 'tp')
- key_grad: bfloat16 [8192, 4096], P('ctx', 'tp')
- value_grad: bfloat16 [8192, 4096], P('ctx', 'tp')
- filter_grad: float32 [8192, 4096], P('ctx', 'tp')
- taps_grad: float32 [3, 3, 4096], P(None, None, 'tp')
The draws below stay inside these ranges and needn't reach their ends.
All inputs are finite; a program needn't handle non-finite values.
Results may differ from the reference program's by a relative error of at most 0.001.
Values may be sent and summed in bfloat16 or wider, within the bound.
A program may use at most 64 MiB of HBM per device.

```python
import math
import jax
import jax.numpy as jnp
from jax import lax

FEATURE_COUNT = 4096
KT = 3
STEP_TOTAL = 8192


def draw_long_filter(key, part):
    key_span = jax.random.fold_in(key, 11)
    key_noise = jax.random.fold_in(key, 12)
    key_marks = jax.random.fold_in(key, 13)
    key_drops = jax.random.fold_in(key, 14)
    fading_span = jnp.exp(jax.random.uniform(key_span, (1, FEATURE_COUNT), jnp.float32, math.log(30.0), math.log(4.0 * STEP_TOTAL)))
    jagged_perturbation = jnp.clip(jax.random.normal(key_noise, (STEP_TOTAL, FEATURE_COUNT), jnp.float32), -4.0, 4.0)
    element_indices = jnp.arange(STEP_TOTAL, dtype=jnp.int32)[:, None]
    place_labels = jax.random.randint(key_marks, (4,), 0, STEP_TOTAL)
    fading_falloff = jax.random.uniform(key_drops, (4, FEATURE_COUNT), jnp.float32, 0.5, 0.8)
    random_spike = jnp.ones((STEP_TOTAL, FEATURE_COUNT), jnp.float32)
    for partner_rank in range(4):
        random_spike = random_spike * jnp.where(element_indices >= place_labels[partner_rank], fading_falloff[partner_rank][None, :], 1.0)
    kernel_magnitude = jnp.sqrt(jnp.expm1(-2.0 / fading_span) / jnp.expm1(-2.0 * STEP_TOTAL / fading_span))
    lag_amount_shift = element_indices.astype(jnp.float32)
    return (jagged_perturbation * jnp.exp(-lag_amount_shift / fading_span) * random_spike * kernel_magnitude).astype(jnp.bfloat16)


def block_levels(key, dims, cuts, smallest, top_value):
    def one(axis_at, parts):
        heights = jax.random.uniform(jax.random.fold_in(jax.random.fold_in(key, 6), axis_at), (parts,), jnp.float32, smallest / len(cuts), top_value / len(cuts))
        return jnp.repeat(jnp.exp(heights), dims[axis_at] // parts).reshape((-1,) + (1,) * (len(dims) - axis_at - 1))

    loudness = one(*cuts[0])
    for cut in cuts[1:]:
        loudness = loudness * one(*cut)
    return loudness


def bell_draw(key, shape, width, bound, pieces=(), held_as=jnp.bfloat16):
    values = jax.random.normal(key, shape, jnp.float32) * width
    if len(pieces) > 0:
        values = block_levels(key, shape, pieces, -0.22, 0.18) * values
    return jnp.clip(values, min=-bound, max=bound).astype(held_as)


def setup_inputs(seed: int = 0) -> dict:
    key_of = jax.random.split(jax.random.key(seed), 7)
    query_in = bell_draw(key_of[0], (STEP_TOTAL, FEATURE_COUNT), 1.0, 6.0, ((0, 64), (1, 16)))
    key_in = bell_draw(key_of[1], (STEP_TOTAL, FEATURE_COUNT), 1.0, 6.0, ((0, 64), (1, 16)))
    value_in = bell_draw(key_of[2], (STEP_TOTAL, FEATURE_COUNT), 1.0, 6.0, ((0, 64), (1, 16)))
    long_filter = draw_long_filter(jax.random.fold_in(key_of[6], 71), 0)
    short_taps = bell_draw(key_of[4], (3, KT, FEATURE_COUNT), KT ** -0.5, 3.5, ((2, 16),))
    out_grad = bell_draw(key_of[5], (STEP_TOTAL, FEATURE_COUNT), 1.0, 6.0, ((0, 64), (1, 16)))
    return dict(query_in=query_in, key_in=key_in, value_in=value_in, long_filter=long_filter, short_taps=short_taps, out_grad=out_grad)


def short_filter(padded, tap_gain, row_count):
    margin = tap_gain.shape[0] - 1
    running = tap_gain[0] * padded[margin:margin + row_count]
    for offset in range(1, margin + 1):
        running = running + tap_gain[offset] * padded[margin - offset:margin - offset + row_count]
    return running

def one_block(operands):
    query_in, key_in, value_in, long_filter, short_taps, out_grad = operands
    row_count = query_in.shape[0]
    margin = short_taps.shape[1] - 1
    tap_gain = short_taps.astype(jnp.float32)
    padded = [jnp.pad(source.astype(jnp.float32), ((margin, 0), (0, 0))) for source in (query_in, key_in, value_in)]
    filtered = [short_filter(padded[partner_rank], tap_gain[partner_rank], row_count) for partner_rank in range(3)]
    mixed_in = filtered[1] * filtered[2]
    length = 2 * row_count
    mixed_spec = jnp.fft.rfft(mixed_in, n=length, axis=0)
    filter_spec = jnp.fft.rfft(long_filter.astype(jnp.float32), n=length, axis=0)
    convolved = jnp.fft.irfft(mixed_spec * filter_spec, n=length, axis=0)[:row_count]
    output = (filtered[0] * convolved).astype(jnp.bfloat16)
    grad_in = out_grad.astype(jnp.float32)
    gate_grad = grad_in * convolved
    conv_grad = grad_in * filtered[0]
    grad_spec = jnp.fft.rfft(conv_grad, n=length, axis=0)
    mixed_grad = jnp.fft.irfft(grad_spec * jnp.conj(filter_spec), n=length, axis=0)[:row_count]
    grad_scale = 1.0 / math.sqrt(row_count)
    filter_grad = jnp.fft.irfft(grad_spec * jnp.conj(mixed_spec), n=length, axis=0)[:row_count] * grad_scale
    inner_grads = [gate_grad, mixed_grad * filtered[2], mixed_grad * filtered[1]]
    input_grads = []
    tap_grads = []
    for partner_rank in range(3):
        padded_grad = jnp.pad(inner_grads[partner_rank], ((0, margin), (0, 0)))
        running = tap_gain[partner_rank, 0] * inner_grads[partner_rank]
        for offset in range(1, margin + 1):
            running = running + tap_gain[partner_rank, offset] * padded_grad[offset:offset + row_count]
        input_grads.append(running.astype(jnp.bfloat16))
        tap_grads.append(jnp.stack([lax.optimization_barrier(jnp.sum(inner_grads[partner_rank] * padded[partner_rank][margin - offset:margin - offset + row_count], axis=0)) for offset in range(margin + 1)]))
    return (output, input_grads[0], input_grads[1], input_grads[2], filter_grad, jnp.stack(tap_grads) * grad_scale)

def reference(query_in, key_in, value_in, long_filter, short_taps, out_grad):
    row_count, channels = query_in.shape
    block_width = math.gcd(channels, 256)
    block_count = channels // block_width

    def to_blocks(array):
        return array.reshape(row_count, block_count, block_width).transpose(1, 0, 2)

    def from_blocks(array):
        return array.transpose(1, 0, 2).reshape(row_count, channels)
    tap_blocks = short_taps.reshape(3, KT, block_count, block_width).transpose(2, 0, 1, 3)
    results = lax.map(one_block, (to_blocks(query_in), to_blocks(key_in), to_blocks(value_in), to_blocks(long_filter), tap_blocks, to_blocks(out_grad)))
    taps_grad = results[5].transpose(1, 2, 0, 3).reshape(3, KT, channels)
    return (from_blocks(results[0]), from_blocks(results[1]), from_blocks(results[2]), from_blocks(results[3]), from_blocks(results[4]), taps_grad)
```

```python
import math

import jax
import jax.numpy as jnp
import ml_dtypes
import numpy as np
from jax import lax
from jax.experimental import pallas as pl
from jax.experimental.pallas import tpu as pltpu
from jax.sharding import PartitionSpec as P

F32 = jnp.float32
BF16 = jnp.bfloat16


def split_np(table):
    high = table.astype(np.float32).astype(ml_dtypes.bfloat16)
    low = (table - high.astype(np.float64)).astype(np.float32).astype(ml_dtypes.bfloat16)
    return high, low


def transform_tables(blocks, width):
    length = blocks * width
    k1 = np.arange(blocks)[:, None] + 0.25
    s = np.arange(blocks)[None, :]
    p = np.arange(width)[None, :]
    angle = 2.0 * np.pi * k1 * s / blocks
    high, low = split_np(np.concatenate([np.cos(angle), -np.sin(angle)], axis=0))
    first = np.concatenate([high, low, high], axis=1)
    twist_angle = 2.0 * np.pi * k1 * p / length
    twist = np.stack([np.cos(twist_angle), -np.sin(twist_angle)]).astype(np.float32)
    p_col = np.arange(width)[:, None]
    k2 = np.arange(width)[None, :]
    angle2 = 2.0 * np.pi * (p_col * k2 % width) / width
    cosine, sine = np.cos(angle2), np.sin(angle2)
    second = np.stack(split_np(np.block([[cosine, -sine], [sine, cosine]])))
    second_back = np.stack(split_np(np.block([[cosine, sine], [-sine, cosine]])))
    high, low = split_np(np.concatenate([np.cos(angle).T, -np.sin(angle).T], axis=1) / length)
    first_back = np.concatenate([high, low, high], axis=1)
    return first, twist, second, second_back, first_back


def halves(x):
    high = x.astype(BF16)
    low = (x - high.astype(F32)).astype(BF16)
    return high, low


def dot(a, b):
    return jnp.dot(a, b, preferred_element_type=F32)


def later(x, offset, lane, row):
    turned = pltpu.roll(x, offset, 1)
    above = jnp.where(row == 0, 0.0, pltpu.roll(turned, 1, 0))
    return jnp.where(lane < offset, above, turned)


def sooner(x, offset, lane, row):
    rows, width = x.shape
    turned = pltpu.roll(x, width - offset, 1)
    below = jnp.where(row == rows - 1, 0.0, pltpu.roll(turned, rows - 1, 0))
    return jnp.where(lane >= width - offset, below, turned)


def layer(load, taps, first, twist, second, second_back, first_back, store, store_sums, channels):
    width = 128
    rows = twist.shape[1]
    lane = lax.broadcasted_iota(jnp.int32, (rows, width), 1)
    row = lax.broadcasted_iota(jnp.int32, (rows, width), 0)
    shifted = {}
    filtered = {}
    for c in range(channels):
        for i in range(3):
            x = load(i, c)
            shifted[i, c] = [x, later(x, 1, lane, row), later(x, 2, lane, row)]
            filtered[i, c] = sum(taps(i, j, c) * shifted[i, c][j] for j in range(3))
    grads = [load(3, c) for c in range(channels)]
    signals = []
    for c in range(channels):
        signals += [filtered[1, c] * filtered[2, c], grads[c] * filtered[0, c]]
    high, low = halves(jnp.concatenate(signals, axis=1))
    spread = dot(first, jnp.concatenate([high, high, low], axis=0))
    filt = jnp.concatenate([load(4, c) for c in range(channels)], axis=1).astype(BF16)
    spread_filt = dot(first[:, : 2 * rows], jnp.concatenate([filt, filt], axis=0))
    turned = []
    for j in range(3 * channels):
        source, at = (spread, j) if j < 2 * channels else (spread_filt, j - 2 * channels)
        re = source[:rows, at * width : (at + 1) * width]
        im = source[rows:, at * width : (at + 1) * width]
        turned.append(jnp.concatenate([re * twist[0] - im * twist[1], re * twist[1] + im * twist[0]], axis=1))
    high, low = halves(jnp.concatenate(turned, axis=0))
    spectra = dot(high, second[0]) + dot(low, second[0]) + dot(high, second[1])

    def spectrum(j):
        block = spectra[j * rows : (j + 1) * rows]
        return block[:, :width], block[:, width:]

    products = []
    for c in range(channels):
        mr, mi = spectrum(2 * c)
        gr, gi = spectrum(2 * c + 1)
        hr, hi = spectrum(2 * channels + c)
        products.append(jnp.concatenate([mr * hr - mi * hi, mr * hi + mi * hr], axis=1))
        products.append(jnp.concatenate([gr * hr + gi * hi, gi * hr - gr * hi], axis=1))
        products.append(jnp.concatenate([gr * mr + gi * mi, gi * mr - gr * mi], axis=1))
    high, low = halves(jnp.concatenate(products, axis=0))
    back = dot(high, second_back[0]) + dot(low, second_back[0]) + dot(high, second_back[1])
    columns = []
    for j in range(3 * channels):
        re = back[j * rows : (j + 1) * rows, :width]
        im = back[j * rows : (j + 1) * rows, width:]
        columns.append(jnp.concatenate([re * twist[0] + im * twist[1], im * twist[0] - re * twist[1]], axis=0))
    high, low = halves(jnp.concatenate(columns, axis=1))
    result = dot(first_back, jnp.concatenate([high, high, low], axis=0))
    scale = 1.0 / math.sqrt(rows * width)
    sums = []
    for c in range(channels):
        convolved, mixed_grad, filter_grad = (
            result[:, (3 * c + j) * width : (3 * c + j + 1) * width] for j in range(3)
        )
        store(0, c, filtered[0, c] * convolved)
        inner = [grads[c] * convolved, mixed_grad * filtered[2, c], mixed_grad * filtered[1, c]]
        for i in range(3):
            g = inner[i]
            grad = taps(i, 0, c) * g + taps(i, 1, c) * sooner(g, 1, lane, row) + taps(i, 2, c) * sooner(g, 2, lane, row)
            store(1 + i, c, grad)
            for j in range(3):
                sums.append(((i, j, c), jnp.sum(g * shifted[i, c][j], axis=0, keepdims=True) * scale))
        store(4, c, filter_grad * scale)
    store_sums(sums)


def layer_kernel(channels, x_ref, taps_ref, first_ref, twist_ref, second_ref, back_ref, first_back_ref, out_ref, grad_ref, sums_ref):
    def load(a, c):
        return x_ref[a * channels + c].astype(F32)

    def taps(i, j, c):
        return taps_ref[(i * 3 + j) * channels + c]

    def store(a, c, value):
        if a < 4:
            out_ref[a * channels + c] = value.astype(BF16)
        else:
            grad_ref[c] = value

    def store_sums(sums):
        for (i, j, c), value in sums:
            at = (i * 3 + j) * channels + c
            sums_ref[at : at + 1, :] = value

    layer(load, taps, first_ref[...], twist_ref[...], second_ref[...], back_ref[...], first_back_ref[...], store, store_sums, channels)


def local(query_in, key_in, value_in, long_filter, short_taps, out_grad):
    rows, width = query_in.shape
    parts = lax.axis_size("ctx")
    me = lax.axis_index("ctx")
    channels = width // parts
    tables = [jnp.asarray(t) for t in transform_tables(parts, rows)]
    inputs = jnp.stack([query_in, key_in, value_in, out_grad, long_filter])
    outgoing = inputs.reshape(5, rows, parts, channels).transpose(2, 0, 3, 1)
    arrived = lax.all_to_all(outgoing, "ctx", split_axis=0, concat_axis=0, tiled=True)
    signals = arrived.transpose(1, 2, 0, 3).reshape(5 * channels, parts, rows)
    my_taps = lax.dynamic_slice_in_dim(short_taps, me * channels, channels, 2).astype(F32).reshape(-1)
    vmem = pl.BlockSpec(memory_space=pltpu.VMEM)
    out, grad, sums = pl.pallas_call(
        lambda *refs: layer_kernel(channels, *refs),
        out_shape=(
            jax.ShapeDtypeStruct((4 * channels, parts, rows), BF16),
            jax.ShapeDtypeStruct((channels, parts, rows), F32),
            jax.ShapeDtypeStruct((9 * channels, rows), F32),
        ),
        in_specs=[vmem, pl.BlockSpec(memory_space=pltpu.SMEM)] + [vmem] * 5,
        out_specs=(vmem, vmem, vmem),
        name="layer",
    )(signals, my_taps, *tables)
    sums = jnp.sum(sums, axis=1)
    sums = jnp.broadcast_to(jnp.pad(sums, (0, rows - sums.shape[0]))[None, None, :], (1, parts, rows))
    wide = jnp.concatenate([grad, sums], axis=0)
    high = lax.reduce_precision(wide, 8, 7)
    low = wide - high
    returning = jnp.concatenate([out, high.astype(BF16), low.astype(BF16)], axis=0).transpose(1, 0, 2)
    returned = lax.all_to_all(returning, "ctx", split_axis=0, concat_axis=0, tiled=True)
    fields = returned[:, : 4 * channels].reshape(parts, 4, channels, rows)
    fields = fields.transpose(1, 3, 0, 2).reshape(4, rows, width)
    high = returned[:, 4 * channels : 5 * channels + 1].astype(F32)
    low = returned[:, 5 * channels + 1 : 6 * channels + 2].astype(F32)
    wide = high + low
    filter_grad = wide[:, :channels].transpose(2, 0, 1).reshape(rows, width)
    taps_grad = wide[:, channels, : 9 * channels].reshape(parts, 3, 3, channels)
    taps_grad = taps_grad.transpose(1, 2, 0, 3).reshape(3, 3, width)
    return fields[0], fields[1], fields[2], fields[3], filter_grad, taps_grad


def solution(mesh):
    placed = P("ctx", "tp")
    taps_placed = P(None, None, "tp")
    return jax.shard_map(
        local,
        mesh=mesh,
        in_specs=(placed, placed, placed, placed, taps_placed, placed),
        out_specs=(placed, placed, placed, placed, placed, taps_placed),
        check_vma=False,
    )
```

```python
import math

import jax
import jax.numpy as jnp
import ml_dtypes
import numpy as np
from jax import lax
from jax.experimental import pallas as pl
from jax.experimental.pallas import tpu as pltpu
from jax.sharding import PartitionSpec as P

F32 = jnp.float32
BF16 = jnp.bfloat16


def split_np(table):
    high = table.astype(np.float32).astype(ml_dtypes.bfloat16)
    low = (table - high.astype(np.float64)).astype(np.float32).astype(ml_dtypes.bfloat16)
    return high, low


def transform_tables(blocks, width):
    length = blocks * width
    k1 = np.arange(blocks)[:, None] + 0.25
    s = np.arange(blocks)[None, :]
    p = np.arange(width)[None, :]
    angle = 2.0 * np.pi * k1 * s / blocks
    high, low = split_np(np.concatenate([np.cos(angle), -np.sin(angle)], axis=0))
    first = np.concatenate([high, low, high], axis=1)
    twist_angle = 2.0 * np.pi * k1 * p / length
    twist = np.stack([np.cos(twist_angle), -np.sin(twist_angle)]).astype(np.float32)
    p_col = np.arange(width)[:, None]
    k2 = np.arange(width)[None, :]
    angle2 = 2.0 * np.pi * (p_col * k2 % width) / width
    cosine, sine = np.cos(angle2), np.sin(angle2)
    second = np.stack(split_np(np.block([[cosine, -sine], [sine, cosine]])))
    second_back = np.stack(split_np(np.block([[cosine, sine], [-sine, cosine]])))
    high, low = split_np(np.concatenate([np.cos(angle).T, -np.sin(angle).T], axis=1) / length)
    first_back = np.concatenate([high, low, high], axis=1)
    return first, twist, second, second_back, first_back


def halves(x):
    high = x.astype(BF16)
    low = (x - high.astype(F32)).astype(BF16)
    return high, low


def dot(a, b):
    return jnp.dot(a, b, preferred_element_type=F32)


def later(x, offset, lane, row):
    turned = pltpu.roll(x, offset, 1)
    above = jnp.where(row == 0, 0.0, pltpu.roll(turned, 1, 0))
    return jnp.where(lane < offset, above, turned)


def sooner(x, offset, lane, row):
    rows, width = x.shape
    turned = pltpu.roll(x, width - offset, 1)
    below = jnp.where(row == rows - 1, 0.0, pltpu.roll(turned, rows - 1, 0))
    return jnp.where(lane >= width - offset, below, turned)


def layer(load, taps, first, twist, second, second_back, first_back, store, store_sums, channels):
    width = 128
    rows = twist.shape[1]
    lane = lax.broadcasted_iota(jnp.int32, (rows, width), 1)
    row = lax.broadcasted_iota(jnp.int32, (rows, width), 0)
    shifted = {}
    filtered = {}
    for c in range(channels):
        for i in range(3):
            x = load(i, c)
            shifted[i, c] = [x, later(x, 1, lane, row), later(x, 2, lane, row)]
            filtered[i, c] = sum(taps(i, j, c) * shifted[i, c][j] for j in range(3))
    grads = [load(3, c) for c in range(channels)]
    signals = []
    for c in range(channels):
        signals += [filtered[1, c] * filtered[2, c], grads[c] * filtered[0, c]]
    high, low = halves(jnp.concatenate(signals, axis=1))
    spread = dot(first, jnp.concatenate([high, high, low], axis=0))
    filt = jnp.concatenate([load(4, c) for c in range(channels)], axis=1).astype(BF16)
    spread_filt = dot(first[:, : 2 * rows], jnp.concatenate([filt, filt], axis=0))
    turned = []
    for j in range(3 * channels):
        source, at = (spread, j) if j < 2 * channels else (spread_filt, j - 2 * channels)
        re = source[:rows, at * width : (at + 1) * width]
        im = source[rows:, at * width : (at + 1) * width]
        turned.append(jnp.concatenate([re * twist[0] - im * twist[1], re * twist[1] + im * twist[0]], axis=1))
    high, low = halves(jnp.concatenate(turned, axis=0))
    spectra = dot(high, second[0]) + dot(low, second[0]) + dot(high, second[1])

    def spectrum(j):
        block = spectra[j * rows : (j + 1) * rows]
        return block[:, :width], block[:, width:]

    products = []
    for c in range(channels):
        mr, mi = spectrum(2 * c)
        gr, gi = spectrum(2 * c + 1)
        hr, hi = spectrum(2 * channels + c)
        products.append(jnp.concatenate([mr * hr - mi * hi, mr * hi + mi * hr], axis=1))
        products.append(jnp.concatenate([gr * hr + gi * hi, gi * hr - gr * hi], axis=1))
        products.append(jnp.concatenate([gr * mr + gi * mi, gi * mr - gr * mi], axis=1))
    high, low = halves(jnp.concatenate(products, axis=0))
    back = dot(high, second_back[0]) + dot(low, second_back[0]) + dot(high, second_back[1])
    columns = []
    for j in range(3 * channels):
        re = back[j * rows : (j + 1) * rows, :width]
        im = back[j * rows : (j + 1) * rows, width:]
        columns.append(jnp.concatenate([re * twist[0] + im * twist[1], im * twist[0] - re * twist[1]], axis=0))
    high, low = halves(jnp.concatenate(columns, axis=1))
    result = dot(first_back, jnp.concatenate([high, high, low], axis=0))
    scale = 1.0 / math.sqrt(rows * width)
    sums = []
    for c in range(channels):
        convolved, mixed_grad, filter_grad = (
            result[:, (3 * c + j) * width : (3 * c + j + 1) * width] for j in range(3)
        )
        store(0, c, filtered[0, c] * convolved)
        inner = [grads[c] * convolved, mixed_grad * filtered[2, c], mixed_grad * filtered[1, c]]
        for i in range(3):
            g = inner[i]
            grad = taps(i, 0, c) * g + taps(i, 1, c) * sooner(g, 1, lane, row) + taps(i, 2, c) * sooner(g, 2, lane, row)
            store(1 + i, c, grad)
            for j in range(3):
                sums.append(((i, j, c), jnp.sum(g * shifted[i, c][j], axis=0, keepdims=True) * scale))
        store(4, c, filter_grad * scale)
    store_sums(sums)


MESH = pl.DeviceIdType.MESH


def partner(me, step, parts):
    cores, across = 2, 8 if parts == 64 else parts // 4
    far = parts // (cores * across)
    core, z, x = me % cores, (me // cores) % across, me // (cores * across)
    group = cores * far
    turn, rest = step // group, group - 1 - step % group
    shift = across // 2 + (1 - 2 * (turn % 2)) * ((turn + 1) // 2)
    z_to = (z + shift + across) % across
    return ((x + rest // cores) % far) * (cores * across) + z_to * cores + (core + rest % cores) % cores


def exchange_kernel(parts, channels, q_hbm, k_hbm, v_hbm, g_hbm, h_hbm, taps_ref, first_hbm, twist_hbm, second_hbm, back_hbm, first_back_hbm,
                    got_ref, got_wide_ref, got_sums_ref,
                    raw, first_ref, twist_ref, second_ref, back_ref, first_back_ref, tap_rows, wide, wide_h, sum_rows,
                    send_a, send_h, recv_a, recv_h, send_out, send_wide, send_sums, in_sems, send_sems, recv_sems):
    me = lax.axis_index("ctx")
    fields = 4 * channels
    barrier = pltpu.get_barrier_semaphore()

    def greet(step, carry):
        pl.semaphore_signal(barrier, inc=1, device_id={"ctx": partner(me, step, parts)}, device_id_type=MESH)
        return carry

    lax.fori_loop(0, parts - 1, greet, 0)
    loads = [pltpu.make_async_copy(ref, raw.at[a], in_sems.at[a]) for a, ref in enumerate((q_hbm, k_hbm, v_hbm, g_hbm, h_hbm))]
    pairs = ((first_hbm, first_ref), (twist_hbm, twist_ref), (second_hbm, second_ref), (back_hbm, back_ref), (first_back_hbm, first_back_ref))
    tables = [pltpu.make_async_copy(ref, held, in_sems.at[5 + n]) for n, (ref, held) in enumerate(pairs)]
    for copy in loads + tables:
        copy.start()

    for a in (4, 0, 1, 2, 3):
        loads[a].wait()
        columns = raw[a].astype(F32).T
        for c in range(channels):
            block = columns[c * parts : (c + 1) * parts]
            if a < 4:
                wide[pl.ds(a * channels + c, parts, stride=fields), :] = block
            else:
                wide_h[pl.ds(c, parts, stride=channels), :] = block
        if a == 4:
            for d in range(parts):
                send_h[d] = wide_h[d * channels : (d + 1) * channels, :].astype(BF16)
    send_a[...] = wide[...].astype(BF16)
    lane = lax.broadcasted_iota(jnp.int32, (3, taps_ref.shape[2]), 1)
    for i in range(3):
        taps_i = taps_ref[i].astype(F32)
        for c in range(channels):
            mine = jnp.sum(jnp.where(lane == me + c * parts, taps_i, 0.0), axis=1, keepdims=True)
            tap_rows[c, 3 * i : 3 * i + 3, :] = jnp.broadcast_to(mine, (3, tap_rows.shape[2]))

    pl.semaphore_wait(barrier, parts - 1)

    def block(ref, d, count):
        return ref.at[pl.ds(pl.multiple_of(d * count, count), count)]

    def send(step, carry):
        d = partner(me, step, parts)
        pltpu.make_async_remote_copy(send_h.at[d], recv_h.at[me], send_sems.at[0], recv_sems.at[0], device_id={"ctx": d}, device_id_type=MESH).start()
        pltpu.make_async_remote_copy(block(send_a, d, fields), block(recv_a, me, fields), send_sems.at[1], recv_sems.at[1], device_id={"ctx": d}, device_id_type=MESH).start()
        return carry

    lax.fori_loop(0, parts - 1, send, 0)
    pltpu.make_async_copy(send_h.at[me], recv_h.at[me], recv_sems.at[0]).start()
    pltpu.make_async_copy(block(send_a, me, fields), block(recv_a, me, fields), recv_sems.at[1]).start()
    for copy in tables:
        copy.wait()
    pltpu.make_async_copy(recv_h, recv_h, recv_sems.at[0]).wait()
    pltpu.make_async_copy(recv_a, recv_a, recv_sems.at[1]).wait()

    for d in range(parts):
        wide_h[d * channels : (d + 1) * channels, :] = recv_h[d].astype(F32)
    wide[...] = recv_a[...].astype(F32)

    def load(a, c):
        if a < 4:
            return wide[pl.ds(a * channels + c, parts, stride=fields), :]
        return wide_h[pl.ds(c, parts, stride=channels), :]

    def taps(i, j, c):
        return tap_rows[c, 3 * i + j : 3 * i + j + 1, :]

    def store(a, c, value):
        if a < 4:
            wide[pl.ds(a * channels + c, parts, stride=fields), :] = value
        else:
            wide_h[pl.ds(c, parts, stride=channels), :] = value

    def store_sums(sums):
        sum_rows[...] = jnp.zeros_like(sum_rows)
        for (i, j, c), value in sums:
            at = (i * 3 + j) * channels + c
            sum_rows[at : at + 1, :] = value

    layer(load, taps, first_ref[...], twist_ref, second_ref, back_ref, first_back_ref[...], store, store_sums, channels)
    high, low = halves(sum_rows[...])
    ones = jnp.ones((8, high.shape[1]), BF16)
    along = (((1,), (1,)), ((), ()))
    totals = lax.dot_general(ones, high, along, preferred_element_type=F32) + lax.dot_general(ones, low, along, preferred_element_type=F32)
    send_sums[...] = totals[0:1, :]
    send_out[...] = wide[...].astype(BF16)
    for d in range(parts):
        send_wide[d] = wide_h[d * channels : (d + 1) * channels, :]

    def send_back(step, carry):
        d = partner(me, step, parts)
        pltpu.make_async_remote_copy(block(send_out, d, fields), block(got_ref, me, fields), send_sems.at[2], recv_sems.at[2], device_id={"ctx": d}, device_id_type=MESH).start()
        pltpu.make_async_remote_copy(send_wide.at[d], got_wide_ref.at[me], send_sems.at[3], recv_sems.at[3], device_id={"ctx": d}, device_id_type=MESH).start()
        pltpu.make_async_remote_copy(send_sums, got_sums_ref.at[me], send_sems.at[4], recv_sems.at[4], device_id={"ctx": d}, device_id_type=MESH).start()
        return carry

    lax.fori_loop(0, parts - 1, send_back, 0)
    pltpu.make_async_copy(block(send_out, me, fields), block(got_ref, me, fields), recv_sems.at[2]).start()
    pltpu.make_async_copy(send_wide.at[me], got_wide_ref.at[me], recv_sems.at[3]).start()
    pltpu.make_async_copy(send_sums, got_sums_ref.at[me], recv_sems.at[4]).start()
    others = parts - 1
    pltpu.make_async_copy(recv_h.at[pl.ds(0, others)], recv_h.at[pl.ds(0, others)], send_sems.at[0]).wait()
    for n, ref in ((1, recv_a), (2, got_ref)):
        sent = ref.at[pl.ds(0, others * fields)]
        pltpu.make_async_copy(sent, sent, send_sems.at[n]).wait()
    for n, ref in ((3, got_wide_ref), (4, got_sums_ref)):
        sent = ref.at[pl.ds(0, others)]
        pltpu.make_async_copy(sent, sent, send_sems.at[n]).wait()
    for n, ref in ((2, got_ref), (3, got_wide_ref), (4, got_sums_ref)):
        pltpu.make_async_copy(ref, ref, recv_sems.at[n]).wait()


def finish_kernel(parts, channels, got_ref, got_wide_ref, got_sums_ref, out_ref, q_ref, k_ref, v_ref, h_ref, taps_ref, wide, wide_h, sums, turned):
    fields = 4 * channels
    wide[...] = got_ref[...].astype(F32)
    for a, ref in enumerate((out_ref, q_ref, k_ref, v_ref)):
        blocks = [wide[pl.ds(a * channels + c, parts, stride=fields), :] for c in range(channels)]
        ref[...] = jnp.concatenate(blocks, axis=0).T.astype(BF16)
    sums[...] = jnp.zeros_like(sums)
    for d in range(parts):
        wide_h[d * channels : (d + 1) * channels, :] = got_wide_ref[d]
        sums[d : d + 1, :] = got_sums_ref[d]
    blocks = [wide_h[pl.ds(c, parts, stride=channels), :] for c in range(channels)]
    h_ref[...] = jnp.concatenate(blocks, axis=0).T
    turned[...] = sums[...].T
    rows = jnp.concatenate([turned[pl.ds(c, 16, stride=channels), :][:, :parts] for c in range(channels)], axis=1)
    for i in range(3):
        taps_ref[i] = rows[3 * i : 3 * i + 3]


def local(query_in, key_in, value_in, long_filter, short_taps, out_grad):
    rows, width = query_in.shape
    parts = lax.axis_size("ctx")
    channels = width // parts
    fields = 4 * channels
    tables = [jnp.asarray(t) for t in transform_tables(parts, rows)]
    vmem = pl.BlockSpec(memory_space=pltpu.VMEM)
    hbm = pl.BlockSpec(memory_space=pl.ANY)
    got, got_wide, got_sums = pl.pallas_call(
        lambda *refs: exchange_kernel(parts, channels, *refs),
        out_shape=(
            jax.ShapeDtypeStruct((parts * fields, rows), BF16),
            jax.ShapeDtypeStruct((parts, channels, rows), F32),
            jax.ShapeDtypeStruct((parts, 1, rows), F32),
        ),
        in_specs=[hbm] * 5 + [vmem] + [hbm] * 5,
        out_specs=(vmem, vmem, vmem),
        scratch_shapes=[pltpu.VMEM((5, rows, width), BF16)]
        + [pltpu.VMEM(t.shape, t.dtype) for t in tables]
        + [
            pltpu.VMEM((channels, 16, rows), F32),
            pltpu.VMEM((parts * fields, rows), F32),
            pltpu.VMEM((parts * channels, rows), F32),
            pltpu.VMEM((rows, rows), F32),
            pltpu.VMEM((parts * fields, rows), BF16),
            pltpu.VMEM((parts, channels, rows), BF16),
            pltpu.VMEM((parts * fields, rows), BF16),
            pltpu.VMEM((parts, channels, rows), BF16),
            pltpu.VMEM((parts * fields, rows), BF16),
            pltpu.VMEM((parts, channels, rows), F32),
            pltpu.VMEM((1, rows), F32),
            pltpu.SemaphoreType.DMA((10,)),
            pltpu.SemaphoreType.DMA((5,)),
            pltpu.SemaphoreType.DMA((5,)),
        ],
        compiler_params=pltpu.CompilerParams(collective_id=0, has_side_effects=True),
        name="exchange_and_layer",
    )(query_in, key_in, value_in, out_grad, long_filter, short_taps, *tables)
    field = jax.ShapeDtypeStruct((rows, width), BF16)
    return pl.pallas_call(
        lambda *refs: finish_kernel(parts, channels, *refs),
        out_shape=(field, field, field, field, jax.ShapeDtypeStruct((rows, width), F32), jax.ShapeDtypeStruct(short_taps.shape, F32)),
        in_specs=[vmem] * 3,
        out_specs=(vmem,) * 6,
        scratch_shapes=[
            pltpu.VMEM((parts * fields, rows), F32),
            pltpu.VMEM((parts * channels, rows), F32),
            pltpu.VMEM((rows, rows), F32),
            pltpu.VMEM((rows, rows), F32),
        ],
        name="finish",
    )(got, got_wide, got_sums)


def solution(mesh):
    placed = P("ctx", "tp")
    taps_placed = P(None, None, "tp")
    return jax.shard_map(
        local,
        mesh=mesh,
        in_specs=(placed, placed, placed, placed, taps_placed, placed),
        out_specs=(placed, placed, placed, placed, placed, taps_placed),
        check_vma=False,
    )
```

```python
import math

import jax
import jax.numpy as jnp
import ml_dtypes
import numpy as np
from jax import lax
from jax.experimental import pallas as pl
from jax.experimental.pallas import tpu as pltpu
from jax.sharding import PartitionSpec as P

F32 = jnp.float32
BF16 = jnp.bfloat16


def split_np(table):
    high = table.astype(np.float32).astype(ml_dtypes.bfloat16)
    low = (table - high.astype(np.float64)).astype(np.float32).astype(ml_dtypes.bfloat16)
    return high, low


def transform_tables(blocks, width):
    length = blocks * width
    k1 = np.arange(blocks)[:, None] + 0.25
    s = np.arange(blocks)[None, :]
    p = np.arange(width)[None, :]
    angle = 2.0 * np.pi * k1 * s / blocks
    high, low = split_np(np.concatenate([np.cos(angle), -np.sin(angle)], axis=0))
    first = np.concatenate([high, low, high], axis=1)
    twist_angle = 2.0 * np.pi * k1 * p / length
    twist = np.stack([np.cos(twist_angle), -np.sin(twist_angle)]).astype(np.float32)
    p_col = np.arange(width)[:, None]
    k2 = np.arange(width)[None, :]
    angle2 = 2.0 * np.pi * (p_col * k2 % width) / width
    cosine, sine = np.cos(angle2), np.sin(angle2)
    second = np.stack(split_np(np.block([[cosine, -sine], [sine, cosine]])))
    second_back = np.stack(split_np(np.block([[cosine, sine], [-sine, cosine]])))
    high, low = split_np(np.concatenate([np.cos(angle).T, -np.sin(angle).T], axis=1) / length)
    first_back = np.concatenate([high, low, high], axis=1)
    return first, twist, second, second_back, first_back


def halves(x):
    high = x.astype(BF16)
    low = (x - high.astype(F32)).astype(BF16)
    return high, low


def dot(a, b):
    return jnp.dot(a, b, preferred_element_type=F32)


def later(x, offset, lane, row):
    turned = pltpu.roll(x, offset, 1)
    above = jnp.where(row == 0, 0.0, pltpu.roll(turned, 1, 0))
    return jnp.where(lane < offset, above, turned)


def sooner(x, offset, lane, row):
    rows, width = x.shape
    turned = pltpu.roll(x, width - offset, 1)
    below = jnp.where(row == rows - 1, 0.0, pltpu.roll(turned, rows - 1, 0))
    return jnp.where(lane >= width - offset, below, turned)


def layer(load, taps, first, twist, second, second_back, first_back, store, store_sums, channels):
    width = 128
    rows = twist.shape[1]
    lane = lax.broadcasted_iota(jnp.int32, (rows, width), 1)
    row = lax.broadcasted_iota(jnp.int32, (rows, width), 0)
    shifted = {}
    filtered = {}
    for c in range(channels):
        for i in range(3):
            x = load(i, c)
            shifted[i, c] = [x, later(x, 1, lane, row), later(x, 2, lane, row)]
            filtered[i, c] = sum(taps(i, j, c) * shifted[i, c][j] for j in range(3))
    grads = [load(3, c) for c in range(channels)]
    signals = []
    for c in range(channels):
        signals += [filtered[1, c] * filtered[2, c], grads[c] * filtered[0, c]]
    high, low = halves(jnp.concatenate(signals, axis=1))
    spread = dot(first, jnp.concatenate([high, high, low], axis=0))
    filt = jnp.concatenate([load(4, c) for c in range(channels)], axis=1).astype(BF16)
    spread_filt = dot(first[:, : 2 * rows], jnp.concatenate([filt, filt], axis=0))
    turned = []
    for j in range(3 * channels):
        source, at = (spread, j) if j < 2 * channels else (spread_filt, j - 2 * channels)
        re = source[:rows, at * width : (at + 1) * width]
        im = source[rows:, at * width : (at + 1) * width]
        turned.append(jnp.concatenate([re * twist[0] - im * twist[1], re * twist[1] + im * twist[0]], axis=1))
    high, low = halves(jnp.concatenate(turned, axis=0))
    spectra = dot(high, second[0]) + dot(low, second[0]) + dot(high, second[1])

    def spectrum(j):
        block = spectra[j * rows : (j + 1) * rows]
        return block[:, :width], block[:, width:]

    products = []
    for c in range(channels):
        mr, mi = spectrum(2 * c)
        gr, gi = spectrum(2 * c + 1)
        hr, hi = spectrum(2 * channels + c)
        products.append(jnp.concatenate([mr * hr - mi * hi, mr * hi + mi * hr], axis=1))
        products.append(jnp.concatenate([gr * hr + gi * hi, gi * hr - gr * hi], axis=1))
        products.append(jnp.concatenate([gr * mr + gi * mi, gi * mr - gr * mi], axis=1))
    high, low = halves(jnp.concatenate(products, axis=0))
    back = dot(high, second_back[0]) + dot(low, second_back[0]) + dot(high, second_back[1])
    columns = []
    for j in range(3 * channels):
        re = back[j * rows : (j + 1) * rows, :width]
        im = back[j * rows : (j + 1) * rows, width:]
        columns.append(jnp.concatenate([re * twist[0] + im * twist[1], im * twist[0] - re * twist[1]], axis=0))
    high, low = halves(jnp.concatenate(columns, axis=1))
    result = dot(first_back, jnp.concatenate([high, high, low], axis=0))
    scale = 1.0 / math.sqrt(rows * width)
    sums = []
    for c in range(channels):
        convolved, mixed_grad, filter_grad = (
            result[:, (3 * c + j) * width : (3 * c + j + 1) * width] for j in range(3)
        )
        store(0, c, filtered[0, c] * convolved)
        inner = [grads[c] * convolved, mixed_grad * filtered[2, c], mixed_grad * filtered[1, c]]
        for i in range(3):
            g = inner[i]
            grad = taps(i, 0, c) * g + taps(i, 1, c) * sooner(g, 1, lane, row) + taps(i, 2, c) * sooner(g, 2, lane, row)
            store(1 + i, c, grad)
            for j in range(3):
                sums.append(((i, j, c), jnp.sum(g * shifted[i, c][j], axis=0, keepdims=True) * scale))
        store(4, c, filter_grad * scale)
    store_sums(sums)


MESH = pl.DeviceIdType.MESH
CORES = 2


def exchange_kernel(parts, channels, across, q_hbm, k_hbm, v_hbm, g_hbm, h_hbm, taps_ref, first_hbm, twist_hbm, second_hbm, back_hbm, first_back_hbm,
                    got_ref, got_wide_ref, got_sums_ref,
                    raw, first_ref, twist_ref, second_ref, back_ref, first_back_ref, tap_rows, wide, wide_h, sum_rows,
                    send_a, send_h, recv_a, recv_h, send_out, send_wide, send_sums, line_sums, in_sems, send_sems, recv_sems):
    me = lax.axis_index("ctx")
    batch = channels // 2
    fields = 4 * batch
    others = parts - 1
    far = parts // (CORES * across)
    core, z, x = me % CORES, (me // CORES) % across, me // (CORES * across)
    plane = [((x + j) % far) * (CORES * across) + (core + k) % CORES for j in range(far) for k in range(CORES)]
    plane_index = x * CORES + core

    def each_peer(visit):
        def turn(step, carry):
            shift = across // 2 + (1 - 2 * (step % 2)) * ((step + 1) // 2)
            row = ((z + shift) % across) * CORES
            for base in reversed(plane):
                visit(base + row)
            return carry

        lax.fori_loop(0, across - 1, turn, 0)
        for base in reversed(plane[1:]):
            visit(base + z * CORES)

    def push(source, target, n, d):
        pltpu.make_async_remote_copy(source, target, send_sems.at[n], recv_sems.at[n], device_id={"ctx": d}, device_id_type=MESH).start()

    def keep(source, target, n):
        pltpu.make_async_copy(source, target, recv_sems.at[n]).start()

    def wait_bytes(ref, sem):
        pltpu.make_async_copy(ref, ref, sem).wait()

    barrier = pltpu.get_barrier_semaphore()
    each_peer(lambda d: pl.semaphore_signal(barrier, inc=1, device_id={"ctx": d}, device_id_type=MESH))
    loads = [pltpu.make_async_copy(ref, raw.at[a], in_sems.at[a]) for a, ref in enumerate((q_hbm, k_hbm, v_hbm, g_hbm, h_hbm))]
    pairs = ((first_hbm, first_ref), (twist_hbm, twist_ref), (second_hbm, second_ref), (back_hbm, back_ref), (first_back_hbm, first_back_ref))
    tables = [pltpu.make_async_copy(ref, held, in_sems.at[5 + n]) for n, (ref, held) in enumerate(pairs)]
    for copy in loads + tables:
        copy.start()

    for a in (4, 0, 1, 2, 3):
        loads[a].wait()
        columns = raw[a].astype(F32).T
        for c in range(channels):
            block = columns[c * parts : (c + 1) * parts]
            if a < 4:
                wide[c // batch, pl.ds(a * batch + c % batch, parts, stride=fields), :] = block
            else:
                wide_h[pl.ds(c, parts, stride=channels), :] = block
        if a == 4:
            for d in range(parts):
                send_h[d] = wide_h[d * channels : (d + 1) * channels, :].astype(BF16)
    for b in range(2):
        send_a[b] = wide[b].reshape(parts, fields, wide.shape[2]).astype(BF16)
    lane = lax.broadcasted_iota(jnp.int32, (3, taps_ref.shape[2]), 1)
    for i in range(3):
        taps_i = taps_ref[i].astype(F32)
        for c in range(channels):
            mine = jnp.sum(jnp.where(lane == me + c * parts, taps_i, 0.0), axis=1, keepdims=True)
            tap_rows[c, 3 * i : 3 * i + 3, :] = jnp.broadcast_to(mine, (3, tap_rows.shape[2]))

    pl.semaphore_wait(barrier, others)

    def send_first(d):
        push(send_h.at[d], recv_h.at[me], 0, d)
        push(send_a.at[0, d], recv_a.at[0, me], 1, d)

    each_peer(send_first)
    each_peer(lambda d: push(send_a.at[1, d], recv_a.at[1, me], 2, d))
    keep(send_h.at[me], recv_h.at[me], 0)
    for b in range(2):
        keep(send_a.at[b, me], recv_a.at[b, me], 1 + b)
    for copy in tables:
        copy.wait()
    sum_rows[...] = jnp.zeros_like(sum_rows)

    def run(b):
        if b == 0:
            wait_bytes(recv_h, recv_sems.at[0])
            for d in range(parts):
                wide_h[d * channels : (d + 1) * channels, :] = recv_h[d].astype(F32)
        wait_bytes(recv_a.at[b], recv_sems.at[1 + b])
        wide[b] = recv_a[b].astype(F32).reshape(parts * fields, wide.shape[2])

        def load(a, c):
            if a < 4:
                return wide[b, pl.ds(a * batch + c, parts, stride=fields), :]
            return wide_h[pl.ds(b * batch + c, parts, stride=channels), :]

        def taps(i, j, c):
            return tap_rows[b * batch + c, 3 * i + j : 3 * i + j + 1, :]

        def store(a, c, value):
            if a < 4:
                wide[b, pl.ds(a * batch + c, parts, stride=fields), :] = value
            else:
                wide_h[pl.ds(b * batch + c, parts, stride=channels), :] = value

        def store_sums(sums):
            for (i, j, c), value in sums:
                at = (i * 3 + j) * channels + b * batch + c
                sum_rows[at : at + 1, :] = value

        layer(load, taps, first_ref[...], twist_ref, second_ref, back_ref, first_back_ref[...], store, store_sums, batch)
        send_out[b] = wide[b].reshape(parts, fields, wide.shape[2]).astype(BF16)

    run(0)
    each_peer(lambda d: push(send_out.at[0, d], got_ref.at[0, me], 3, d))
    keep(send_out.at[0, me], got_ref.at[0, me], 3)
    run(1)
    high, low = halves(sum_rows[...])
    ones = jnp.ones((8, high.shape[1]), BF16)
    along = (((1,), (1,)), ((), ()))
    totals = lax.dot_general(ones, high, along, preferred_element_type=F32) + lax.dot_general(ones, low, along, preferred_element_type=F32)
    send_sums[...] = totals[0:1, :]
    for d in range(parts):
        send_wide[d] = wide_h[d * channels : (d + 1) * channels, :]
    for k in range(1, across):
        push(send_sums, line_sums.at[z], 6, plane[0] + ((z + k) % across) * CORES)
    keep(send_sums, line_sums.at[z], 6)

    def send_last(d):
        push(send_out.at[1, d], got_ref.at[1, me], 4, d)
        push(send_wide.at[d], got_wide_ref.at[me], 5, d)

    each_peer(send_last)
    keep(send_out.at[1, me], got_ref.at[1, me], 4)
    keep(send_wide.at[me], got_wide_ref.at[me], 5)
    wait_bytes(line_sums, recv_sems.at[6])
    for base in plane[1:]:
        push(line_sums, got_sums_ref.at[plane_index], 7, base + z * CORES)
    keep(line_sums, got_sums_ref.at[plane_index], 7)
    for n, ref in enumerate((recv_h, recv_a.at[0], recv_a.at[1], got_ref.at[0], got_ref.at[1], got_wide_ref, line_sums, got_sums_ref)):
        sent = ref.at[pl.ds(0, ref.shape[0] - 1)]
        wait_bytes(sent, send_sems.at[n])
    for n, ref in ((3, got_ref.at[0]), (4, got_ref.at[1]), (5, got_wide_ref), (7, got_sums_ref)):
        wait_bytes(ref, recv_sems.at[n])


def finish_kernel(parts, channels, across, got_ref, got_wide_ref, got_sums_ref, out_ref, q_ref, k_ref, v_ref, h_ref, taps_ref, wide, wide_h, sums, turned):
    batch = channels // 2
    fields = 4 * batch
    for b in range(2):
        wide[b] = got_ref[b].astype(F32).reshape(parts * fields, wide.shape[2])
    for a, ref in enumerate((out_ref, q_ref, k_ref, v_ref)):
        blocks = [wide[c // batch, pl.ds(a * batch + c % batch, parts, stride=fields), :] for c in range(channels)]
        ref[...] = jnp.concatenate(blocks, axis=0).T.astype(BF16)
    sums[...] = jnp.zeros_like(sums)
    for d in range(parts):
        wide_h[d * channels : (d + 1) * channels, :] = got_wide_ref[d]
        at = d // (CORES * across) * CORES + d % CORES
        sums[d : d + 1, :] = got_sums_ref[at, (d // CORES) % across]
    blocks = [wide_h[pl.ds(c, parts, stride=channels), :] for c in range(channels)]
    h_ref[...] = jnp.concatenate(blocks, axis=0).T
    turned[...] = sums[...].T
    rows = jnp.concatenate([turned[pl.ds(c, 16, stride=channels), :][:, :parts] for c in range(channels)], axis=1)
    for i in range(3):
        taps_ref[i] = rows[3 * i : 3 * i + 3]


def local(query_in, key_in, value_in, long_filter, short_taps, out_grad):
    rows, width = query_in.shape
    parts = lax.axis_size("ctx")
    across = 8 if parts == 64 else parts // 4
    channels = width // parts
    fields = 2 * channels
    tables = [jnp.asarray(t) for t in transform_tables(parts, rows)]
    vmem = pl.BlockSpec(memory_space=pltpu.VMEM)
    hbm = pl.BlockSpec(memory_space=pl.ANY)
    planes = parts // across
    both = (2, parts, fields, rows)
    got = pl.pallas_call(
        lambda *refs: exchange_kernel(parts, channels, across, *refs),
        out_shape=(
            jax.ShapeDtypeStruct(both, BF16),
            jax.ShapeDtypeStruct((parts, channels, rows), F32),
            jax.ShapeDtypeStruct((planes, across, 1, rows), F32),
        ),
        in_specs=[hbm] * 5 + [vmem] + [hbm] * 5,
        out_specs=(vmem, vmem, vmem),
        scratch_shapes=[pltpu.VMEM((5, rows, width), BF16)]
        + [pltpu.VMEM(t.shape, t.dtype) for t in tables]
        + [
            pltpu.VMEM((channels, 16, rows), F32),
            pltpu.VMEM((2, parts * fields, rows), F32),
            pltpu.VMEM((parts * channels, rows), F32),
            pltpu.VMEM((rows, rows), F32),
            pltpu.VMEM(both, BF16),
            pltpu.VMEM((parts, channels, rows), BF16),
            pltpu.VMEM(both, BF16),
            pltpu.VMEM((parts, channels, rows), BF16),
            pltpu.VMEM(both, BF16),
            pltpu.VMEM((parts, channels, rows), F32),
            pltpu.VMEM((1, rows), F32),
            pltpu.VMEM((across, 1, rows), F32),
            pltpu.SemaphoreType.DMA((10,)),
            pltpu.SemaphoreType.DMA((8,)),
            pltpu.SemaphoreType.DMA((8,)),
        ],
        compiler_params=pltpu.CompilerParams(collective_id=0, has_side_effects=True),
        name="exchange_and_layer",
    )(query_in, key_in, value_in, out_grad, long_filter, short_taps, *tables)
    field = jax.ShapeDtypeStruct((rows, width), BF16)
    return pl.pallas_call(
        lambda *refs: finish_kernel(parts, channels, across, *refs),
        out_shape=(field, field, field, field, jax.ShapeDtypeStruct((rows, width), F32), jax.ShapeDtypeStruct(short_taps.shape, F32)),
        in_specs=[vmem] * 3,
        out_specs=(vmem,) * 6,
        scratch_shapes=[
            pltpu.VMEM((2, parts * fields, rows), F32),
            pltpu.VMEM((parts * channels, rows), F32),
            pltpu.VMEM((rows, rows), F32),
            pltpu.VMEM((rows, rows), F32),
        ],
        name="finish",
    )(*got)


def solution(mesh):
    placed = P("ctx", "tp")
    taps_placed = P(None, None, "tp")
    return jax.shard_map(
        local,
        mesh=mesh,
        in_specs=(placed, placed, placed, placed, taps_placed, placed),
        out_specs=(placed, placed, placed, placed, placed, taps_placed),
        check_vma=False,
    )
```

```python
import math

import jax
import jax.numpy as jnp
import ml_dtypes
import numpy as np
from jax import lax
from jax.experimental import pallas as pl
from jax.experimental.pallas import tpu as pltpu
from jax.sharding import PartitionSpec as P

F32 = jnp.float32
BF16 = jnp.bfloat16


def split_np(table):
    high = table.astype(np.float32).astype(ml_dtypes.bfloat16)
    low = (table - high.astype(np.float64)).astype(np.float32).astype(ml_dtypes.bfloat16)
    return high, low


def transform_tables(blocks, width):
    length = blocks * width
    k1 = np.arange(blocks)[:, None] + 0.25
    s = np.arange(blocks)[None, :]
    p = np.arange(width)[None, :]
    angle = 2.0 * np.pi * k1 * s / blocks
    high, low = split_np(np.concatenate([np.cos(angle), -np.sin(angle)], axis=0))
    first = np.concatenate([high, low, high], axis=1)
    twist_angle = 2.0 * np.pi * k1 * p / length
    twist = np.stack([np.cos(twist_angle), -np.sin(twist_angle)]).astype(np.float32)
    p_col = np.arange(width)[:, None]
    k2 = np.arange(width)[None, :]
    angle2 = 2.0 * np.pi * (p_col * k2 % width) / width
    cosine, sine = np.cos(angle2), np.sin(angle2)
    second = np.stack(split_np(np.block([[cosine, -sine], [sine, cosine]])))
    second_back = np.stack(split_np(np.block([[cosine, sine], [-sine, cosine]])))
    high, low = split_np(np.concatenate([np.cos(angle).T, -np.sin(angle).T], axis=1) / length)
    first_back = np.concatenate([high, low, high], axis=1)
    return first, twist, second, second_back, first_back


def halves(x):
    high = x.astype(BF16)
    low = (x - high.astype(F32)).astype(BF16)
    return high, low


def dot(a, b):
    return jnp.dot(a, b, preferred_element_type=F32)


def later(x, offset, lane, row):
    turned = pltpu.roll(x, offset, 1)
    above = jnp.where(row == 0, 0.0, pltpu.roll(turned, 1, 0))
    return jnp.where(lane < offset, above, turned)


def sooner(x, offset, lane, row):
    rows, width = x.shape
    turned = pltpu.roll(x, width - offset, 1)
    below = jnp.where(row == rows - 1, 0.0, pltpu.roll(turned, rows - 1, 0))
    return jnp.where(lane >= width - offset, below, turned)


def layer(load, taps, first, twist, second, second_back, first_back, store, store_sums, channels):
    width = 128
    rows = twist.shape[1]
    lane = lax.broadcasted_iota(jnp.int32, (rows, width), 1)
    row = lax.broadcasted_iota(jnp.int32, (rows, width), 0)
    shifted = {}
    filtered = {}
    for c in range(channels):
        for i in range(3):
            x = load(i, c)
            shifted[i, c] = [x, later(x, 1, lane, row), later(x, 2, lane, row)]
            filtered[i, c] = sum(taps(i, j, c) * shifted[i, c][j] for j in range(3))
    grads = [load(3, c) for c in range(channels)]
    signals = []
    for c in range(channels):
        signals += [filtered[1, c] * filtered[2, c], grads[c] * filtered[0, c]]
    high, low = halves(jnp.concatenate(signals, axis=1))
    spread = dot(first, jnp.concatenate([high, high, low], axis=0))
    filt = jnp.concatenate([load(4, c) for c in range(channels)], axis=1).astype(BF16)
    spread_filt = dot(first[:, : 2 * rows], jnp.concatenate([filt, filt], axis=0))
    turned = []
    for j in range(3 * channels):
        source, at = (spread, j) if j < 2 * channels else (spread_filt, j - 2 * channels)
        re = source[:rows, at * width : (at + 1) * width]
        im = source[rows:, at * width : (at + 1) * width]
        turned.append(jnp.concatenate([re * twist[0] - im * twist[1], re * twist[1] + im * twist[0]], axis=1))
    high, low = halves(jnp.concatenate(turned, axis=0))
    spectra = dot(high, second[0]) + dot(low, second[0]) + dot(high, second[1])

    def spectrum(j):
        block = spectra[j * rows : (j + 1) * rows]
        return block[:, :width], block[:, width:]

    products = []
    for c in range(channels):
        mr, mi = spectrum(2 * c)
        gr, gi = spectrum(2 * c + 1)
        hr, hi = spectrum(2 * channels + c)
        products.append(jnp.concatenate([mr * hr - mi * hi, mr * hi + mi * hr], axis=1))
        products.append(jnp.concatenate([gr * hr + gi * hi, gi * hr - gr * hi], axis=1))
        products.append(jnp.concatenate([gr * mr + gi * mi, gi * mr - gr * mi], axis=1))
    high, low = halves(jnp.concatenate(products, axis=0))
    back = dot(high, second_back[0]) + dot(low, second_back[0]) + dot(high, second_back[1])
    columns = []
    for j in range(3 * channels):
        re = back[j * rows : (j + 1) * rows, :width]
        im = back[j * rows : (j + 1) * rows, width:]
        columns.append(jnp.concatenate([re * twist[0] + im * twist[1], im * twist[0] - re * twist[1]], axis=0))
    high, low = halves(jnp.concatenate(columns, axis=1))
    result = dot(first_back, jnp.concatenate([high, high, low], axis=0))
    scale = 1.0 / math.sqrt(rows * width)
    sums = []
    for c in range(channels):
        convolved, mixed_grad, filter_grad = (
            result[:, (3 * c + j) * width : (3 * c + j + 1) * width] for j in range(3)
        )
        store(0, c, filtered[0, c] * convolved)
        inner = [grads[c] * convolved, mixed_grad * filtered[2, c], mixed_grad * filtered[1, c]]
        for i in range(3):
            g = inner[i]
            grad = taps(i, 0, c) * g + taps(i, 1, c) * sooner(g, 1, lane, row) + taps(i, 2, c) * sooner(g, 2, lane, row)
            store(1 + i, c, grad)
            for j in range(3):
                sums.append(((i, j, c), jnp.sum(g * shifted[i, c][j], axis=0, keepdims=True) * scale))
        store(4, c, filter_grad * scale)
    store_sums(sums)


MESH = pl.DeviceIdType.MESH
CORES = 2


def exchange_kernel(parts, channels, across, q_hbm, k_hbm, v_hbm, g_hbm, h_hbm, taps_hbm, first_hbm, twist_hbm, second_hbm, back_hbm, first_back_hbm,
                    got_ref, got_wide_ref, got_sums_ref,
                    raw, taps_ref, first_ref, twist_ref, second_ref, back_ref, first_back_ref, tap_rows, wide, wide_h, sum_rows,
                    send_a, send_h, recv_a, recv_h, send_out, send_wide, send_sums, line_sums, in_sems, send_sems, recv_sems):
    me = lax.axis_index("ctx")
    batch = channels // 2
    fields = 4 * batch
    others = parts - 1
    far = parts // (CORES * across)
    core, z, x = me % CORES, (me // CORES) % across, me // (CORES * across)
    plane = [((x + j) % far) * (CORES * across) + (core + k) % CORES for j in range(far) for k in range(CORES)]
    plane_index = x * CORES + core

    def each_peer(visit):
        def turn(step, carry):
            shift = across // 2 + (1 - 2 * (step % 2)) * ((step + 1) // 2)
            row = ((z + shift) % across) * CORES
            for base in reversed(plane):
                visit(base + row)
            return carry

        lax.fori_loop(0, across - 1, turn, 0)
        for base in reversed(plane[1:]):
            visit(base + z * CORES)

    def push(source, target, n, d):
        pltpu.make_async_remote_copy(source, target, send_sems.at[n], recv_sems.at[n], device_id={"ctx": d}, device_id_type=MESH).start()

    def keep(source, target, n):
        pltpu.make_async_copy(source, target, recv_sems.at[n]).start()

    def wait_bytes(ref, sem):
        pltpu.make_async_copy(ref, ref, sem).wait()

    barrier = pltpu.get_barrier_semaphore()
    each_peer(lambda d: pl.semaphore_signal(barrier, inc=1, device_id={"ctx": d}, device_id_type=MESH))
    loads = [pltpu.make_async_copy(ref, raw.at[a], in_sems.at[a]) for a, ref in enumerate((q_hbm, k_hbm, v_hbm, g_hbm, h_hbm))]
    pairs = ((taps_hbm, taps_ref), (first_hbm, first_ref), (twist_hbm, twist_ref), (second_hbm, second_ref), (back_hbm, back_ref), (first_back_hbm, first_back_ref))
    tables = [pltpu.make_async_copy(ref, held, in_sems.at[5 + n]) for n, (ref, held) in enumerate(pairs)]
    for copy in loads + tables:
        copy.start()

    for a in (4, 0, 1, 2, 3):
        loads[a].wait()
        columns = raw[a].astype(F32).T
        for c in range(channels):
            block = columns[c * parts : (c + 1) * parts]
            if a < 4:
                wide[c // batch, pl.ds(a * batch + c % batch, parts, stride=fields), :] = block
            else:
                wide_h[pl.ds(c, parts, stride=channels), :] = block
        if a == 4:
            for d in range(parts):
                send_h[d] = wide_h[d * channels : (d + 1) * channels, :].astype(BF16)
    for b in range(2):
        send_a[b] = wide[b].reshape(parts, fields, wide.shape[2]).astype(BF16)
    tables[0].wait()
    lane = lax.broadcasted_iota(jnp.int32, (3, taps_ref.shape[2]), 1)
    for i in range(3):
        taps_i = taps_ref[i].astype(F32)
        for c in range(channels):
            mine = jnp.sum(jnp.where(lane == me + c * parts, taps_i, 0.0), axis=1, keepdims=True)
            tap_rows[c, 3 * i : 3 * i + 3, :] = jnp.broadcast_to(mine, (3, tap_rows.shape[2]))

    pl.semaphore_wait(barrier, others)

    def send_first(d):
        push(send_h.at[d], recv_h.at[me], 0, d)
        push(send_a.at[0, d], recv_a.at[0, me], 1, d)

    each_peer(send_first)
    each_peer(lambda d: push(send_a.at[1, d], recv_a.at[1, me], 2, d))
    keep(send_h.at[me], recv_h.at[me], 0)
    for b in range(2):
        keep(send_a.at[b, me], recv_a.at[b, me], 1 + b)
    for copy in tables[1:]:
        copy.wait()
    sum_rows[...] = jnp.zeros_like(sum_rows)

    def run(b):
        if b == 0:
            wait_bytes(recv_h, recv_sems.at[0])
            for d in range(parts):
                wide_h[d * channels : (d + 1) * channels, :] = recv_h[d].astype(F32)
        wait_bytes(recv_a.at[b], recv_sems.at[1 + b])
        wide[b] = recv_a[b].astype(F32).reshape(parts * fields, wide.shape[2])

        def load(a, c):
            if a < 4:
                return wide[b, pl.ds(a * batch + c, parts, stride=fields), :]
            return wide_h[pl.ds(b * batch + c, parts, stride=channels), :]

        def taps(i, j, c):
            return tap_rows[b * batch + c, 3 * i + j : 3 * i + j + 1, :]

        def store(a, c, value):
            if a < 4:
                wide[b, pl.ds(a * batch + c, parts, stride=fields), :] = value
            else:
                wide_h[pl.ds(b * batch + c, parts, stride=channels), :] = value

        def store_sums(sums):
            for (i, j, c), value in sums:
                at = (i * 3 + j) * channels + b * batch + c
                sum_rows[at : at + 1, :] = value

        layer(load, taps, first_ref[...], twist_ref, second_ref, back_ref, first_back_ref[...], store, store_sums, batch)
        send_out[b] = wide[b].reshape(parts, fields, wide.shape[2]).astype(BF16)

    run(0)
    each_peer(lambda d: push(send_out.at[0, d], got_ref.at[0, me], 3, d))
    keep(send_out.at[0, me], got_ref.at[0, me], 3)
    run(1)
    high, low = halves(sum_rows[...])
    ones = jnp.ones((8, high.shape[1]), BF16)
    along = (((1,), (1,)), ((), ()))
    totals = lax.dot_general(ones, high, along, preferred_element_type=F32) + lax.dot_general(ones, low, along, preferred_element_type=F32)
    send_sums[...] = totals[0:1, :]
    for d in range(parts):
        send_wide[d] = wide_h[d * channels : (d + 1) * channels, :]
    for k in range(1, across):
        push(send_sums, line_sums.at[z], 6, plane[0] + ((z + k) % across) * CORES)
    keep(send_sums, line_sums.at[z], 6)

    def send_last(d):
        push(send_out.at[1, d], got_ref.at[1, me], 4, d)
        push(send_wide.at[d], got_wide_ref.at[me], 5, d)

    each_peer(send_last)
    keep(send_out.at[1, me], got_ref.at[1, me], 4)
    keep(send_wide.at[me], got_wide_ref.at[me], 5)
    wait_bytes(line_sums, recv_sems.at[6])
    for base in plane[1:]:
        push(line_sums, got_sums_ref.at[plane_index], 7, base + z * CORES)
    keep(line_sums, got_sums_ref.at[plane_index], 7)
    for n, ref in enumerate((recv_h, recv_a.at[0], recv_a.at[1], got_ref.at[0], got_ref.at[1], got_wide_ref, line_sums, got_sums_ref)):
        sent = ref.at[pl.ds(0, ref.shape[0] - 1)]
        wait_bytes(sent, send_sems.at[n])
    for n, ref in ((3, got_ref.at[0]), (4, got_ref.at[1]), (5, got_wide_ref), (7, got_sums_ref)):
        wait_bytes(ref, recv_sems.at[n])


def finish_kernel(parts, channels, across, got_ref, got_wide_ref, got_sums_ref, out_hbm, q_hbm, k_hbm, v_hbm, h_hbm, taps_hbm,
                  wide, wide_h, sums, turned, done, done_h, done_taps, sems):
    batch = channels // 2
    fields = 4 * batch
    copies = []

    def put(source, target):
        copies.append(pltpu.make_async_copy(source, target, sems.at[len(copies)]))
        copies[-1].start()

    for d in range(parts):
        wide_h[d * channels : (d + 1) * channels, :] = got_wide_ref[d]
        at = d // (CORES * across) * CORES + d % CORES
        sums[d : d + 1, :] = got_sums_ref[at, (d // CORES) % across]
    blocks = [wide_h[pl.ds(c, parts, stride=channels), :] for c in range(channels)]
    done_h[...] = jnp.concatenate(blocks, axis=0).T
    put(done_h, h_hbm)
    turned[...] = sums[...].T
    rows = jnp.concatenate([turned[pl.ds(c, 9, stride=channels), :] for c in range(channels)], axis=1)
    for i in range(3):
        done_taps[i] = rows[3 * i : 3 * i + 3]
    put(done_taps, taps_hbm)
    for b in range(2):
        wide[b] = got_ref[b].astype(F32).reshape(parts * fields, wide.shape[2])
    for a, ref in enumerate((out_hbm, q_hbm, k_hbm, v_hbm)):
        blocks = [wide[c // batch, pl.ds(a * batch + c % batch, parts, stride=fields), :] for c in range(channels)]
        done[a] = jnp.concatenate(blocks, axis=0).T.astype(BF16)
        put(done.at[a], ref)
    for copy in copies:
        copy.wait()


def local(query_in, key_in, value_in, long_filter, short_taps, out_grad):
    rows, width = query_in.shape
    parts = lax.axis_size("ctx")
    across = 8 if parts == 64 else parts // 4
    channels = width // parts
    fields = 2 * channels
    tables = [jnp.asarray(t) for t in transform_tables(parts, rows)]
    vmem = pl.BlockSpec(memory_space=pltpu.VMEM)
    hbm = pl.BlockSpec(memory_space=pl.ANY)
    planes = parts // across
    both = (2, parts, fields, rows)
    got = pl.pallas_call(
        lambda *refs: exchange_kernel(parts, channels, across, *refs),
        out_shape=(
            pltpu.VMEM(both, BF16),
            pltpu.VMEM((parts, channels, rows), F32),
            pltpu.VMEM((planes, across, 1, rows), F32),
        ),
        in_specs=[hbm] * 11,
        out_specs=(vmem, vmem, vmem),
        scratch_shapes=[pltpu.VMEM((5, rows, width), BF16), pltpu.VMEM(short_taps.shape, BF16)]
        + [pltpu.VMEM(t.shape, t.dtype) for t in tables]
        + [
            pltpu.VMEM((channels, 16, rows), F32),
            pltpu.VMEM((2, parts * fields, rows), F32),
            pltpu.VMEM((parts * channels, rows), F32),
            pltpu.VMEM((rows, rows), F32),
            pltpu.VMEM(both, BF16),
            pltpu.VMEM((parts, channels, rows), BF16),
            pltpu.VMEM(both, BF16),
            pltpu.VMEM((parts, channels, rows), BF16),
            pltpu.VMEM(both, BF16),
            pltpu.VMEM((parts, channels, rows), F32),
            pltpu.VMEM((1, rows), F32),
            pltpu.VMEM((across, 1, rows), F32),
            pltpu.SemaphoreType.DMA((11,)),
            pltpu.SemaphoreType.DMA((8,)),
            pltpu.SemaphoreType.DMA((8,)),
        ],
        compiler_params=pltpu.CompilerParams(collective_id=0, has_side_effects=True),
        name="exchange_and_layer",
    )(query_in, key_in, value_in, out_grad, long_filter, short_taps, *tables)
    got = [pltpu.with_memory_space_constraint(g, pltpu.VMEM) for g in got]
    field = jax.ShapeDtypeStruct((rows, width), BF16)
    return pl.pallas_call(
        lambda *refs: finish_kernel(parts, channels, across, *refs),
        out_shape=(field, field, field, field, jax.ShapeDtypeStruct((rows, width), F32), jax.ShapeDtypeStruct(short_taps.shape, F32)),
        in_specs=[vmem] * 3,
        out_specs=(hbm,) * 6,
        scratch_shapes=[
            pltpu.VMEM((2, parts * fields, rows), F32),
            pltpu.VMEM((parts * channels, rows), F32),
            pltpu.VMEM((parts, rows), F32),
            pltpu.VMEM((rows, parts), F32),
            pltpu.VMEM((4, rows, width), BF16),
            pltpu.VMEM((rows, width), F32),
            pltpu.VMEM(short_taps.shape, F32),
            pltpu.SemaphoreType.DMA((6,)),
        ],
        name="finish",
    )(*got)


def solution(mesh):
    placed = P("ctx", "tp")
    taps_placed = P(None, None, "tp")
    return jax.shard_map(
        local,
        mesh=mesh,
        in_specs=(placed, placed, placed, placed, taps_placed, placed),
        out_specs=(placed, placed, placed, placed, placed, taps_placed),
        check_vma=False,
    )
```

```python
import math

import jax
import jax.numpy as jnp
import ml_dtypes
import numpy as np
from jax import lax
from jax.experimental import pallas as pl
from jax.experimental.pallas import tpu as pltpu
from jax.sharding import PartitionSpec as P

F32 = jnp.float32
BF16 = jnp.bfloat16


def split_np(table):
    high = table.astype(np.float32).astype(ml_dtypes.bfloat16)
    low = (table - high.astype(np.float64)).astype(np.float32).astype(ml_dtypes.bfloat16)
    return high, low


def transform_tables(blocks, width):
    length = blocks * width
    k1 = np.arange(blocks)[:, None] + 0.25
    s = np.arange(blocks)[None, :]
    p = np.arange(width)[None, :]
    angle = 2.0 * np.pi * k1 * s / blocks
    high, low = split_np(np.concatenate([np.cos(angle), -np.sin(angle)], axis=0))
    first = np.concatenate([high, low, high], axis=1)
    twist_angle = 2.0 * np.pi * k1 * p / length
    twist = np.stack([np.cos(twist_angle), -np.sin(twist_angle)]).astype(np.float32)
    p_col = np.arange(width)[:, None]
    k2 = np.arange(width)[None, :]
    angle2 = 2.0 * np.pi * (p_col * k2 % width) / width
    cosine, sine = np.cos(angle2), np.sin(angle2)
    second = np.stack(split_np(np.block([[cosine, -sine], [sine, cosine]])))
    second_back = np.stack(split_np(np.block([[cosine, sine], [-sine, cosine]])))
    high, low = split_np(np.concatenate([np.cos(angle).T, -np.sin(angle).T], axis=1) / length)
    first_back = np.concatenate([high, low, high], axis=1)
    return first, twist, second, second_back, first_back


def halves(x):
    high = x.astype(BF16)
    low = (x - high.astype(F32)).astype(BF16)
    return high, low


def dot(a, b):
    return jnp.dot(a, b, preferred_element_type=F32)


def later(x, offset, lane, row):
    turned = pltpu.roll(x, offset, 1)
    above = jnp.where(row == 0, 0.0, pltpu.roll(turned, 1, 0))
    return jnp.where(lane < offset, above, turned)


def sooner(x, offset, lane, row):
    rows, width = x.shape
    turned = pltpu.roll(x, width - offset, 1)
    below = jnp.where(row == rows - 1, 0.0, pltpu.roll(turned, rows - 1, 0))
    return jnp.where(lane >= width - offset, below, turned)


def layer(load, taps, first, twist, second, second_back, first_back, store, store_sums, channels):
    width = 128
    rows = twist.shape[1]
    lane = lax.broadcasted_iota(jnp.int32, (rows, width), 1)
    row = lax.broadcasted_iota(jnp.int32, (rows, width), 0)
    shifted = {}
    filtered = {}
    for c in range(channels):
        for i in range(3):
            x = load(i, c)
            shifted[i, c] = [x, later(x, 1, lane, row), later(x, 2, lane, row)]
            filtered[i, c] = sum(taps(i, j, c) * shifted[i, c][j] for j in range(3))
    grads = [load(3, c) for c in range(channels)]
    signals = []
    for c in range(channels):
        signals += [filtered[1, c] * filtered[2, c], grads[c] * filtered[0, c]]
    high, low = halves(jnp.concatenate(signals, axis=1))
    spread = dot(first, jnp.concatenate([high, high, low], axis=0))
    filt = jnp.concatenate([load(4, c) for c in range(channels)], axis=1).astype(BF16)
    spread_filt = dot(first[:, : 2 * rows], jnp.concatenate([filt, filt], axis=0))
    turned = []
    for j in range(3 * channels):
        source, at = (spread, j) if j < 2 * channels else (spread_filt, j - 2 * channels)
        re = source[:rows, at * width : (at + 1) * width]
        im = source[rows:, at * width : (at + 1) * width]
        turned.append(jnp.concatenate([re * twist[0] - im * twist[1], re * twist[1] + im * twist[0]], axis=1))
    high, low = halves(jnp.concatenate(turned, axis=0))
    spectra = dot(high, second[0]) + dot(low, second[0]) + dot(high, second[1])

    def spectrum(j):
        block = spectra[j * rows : (j + 1) * rows]
        return block[:, :width], block[:, width:]

    products = []
    for c in range(channels):
        mr, mi = spectrum(2 * c)
        gr, gi = spectrum(2 * c + 1)
        hr, hi = spectrum(2 * channels + c)
        products.append(jnp.concatenate([mr * hr - mi * hi, mr * hi + mi * hr], axis=1))
        products.append(jnp.concatenate([gr * hr + gi * hi, gi * hr - gr * hi], axis=1))
        products.append(jnp.concatenate([gr * mr + gi * mi, gi * mr - gr * mi], axis=1))
    high, low = halves(jnp.concatenate(products, axis=0))
    back = dot(high, second_back[0]) + dot(low, second_back[0]) + dot(high, second_back[1])
    columns = []
    for j in range(3 * channels):
        re = back[j * rows : (j + 1) * rows, :width]
        im = back[j * rows : (j + 1) * rows, width:]
        columns.append(jnp.concatenate([re * twist[0] + im * twist[1], im * twist[0] - re * twist[1]], axis=0))
    high, low = halves(jnp.concatenate(columns, axis=1))
    result = dot(first_back, jnp.concatenate([high, high, low], axis=0))
    scale = 1.0 / math.sqrt(rows * width)
    sums = []
    for c in range(channels):
        convolved, mixed_grad, filter_grad = (
            result[:, (3 * c + j) * width : (3 * c + j + 1) * width] for j in range(3)
        )
        store(0, c, filtered[0, c] * convolved)
        inner = [grads[c] * convolved, mixed_grad * filtered[2, c], mixed_grad * filtered[1, c]]
        for i in range(3):
            g = inner[i]
            grad = taps(i, 0, c) * g + taps(i, 1, c) * sooner(g, 1, lane, row) + taps(i, 2, c) * sooner(g, 2, lane, row)
            store(1 + i, c, grad)
            for j in range(3):
                sums.append(((i, j, c), jnp.sum(g * shifted[i, c][j], axis=0, keepdims=True) * scale))
        store(4, c, filter_grad * scale)
    store_sums(sums)


MESH = pl.DeviceIdType.MESH
CORES = 2


def exchange_kernel(parts, channels, across, q_hbm, k_hbm, v_hbm, g_hbm, h_hbm, taps_hbm, first_hbm, twist_hbm, second_hbm, back_hbm, first_back_hbm,
                    got_ref, got_wide_ref, got_sums_ref,
                    raw, taps_ref, first_ref, twist_ref, second_ref, back_ref, first_back_ref, tap_rows, wide, wide_h, sum_rows,
                    send_a, send_h, recv_a, recv_h, send_out, send_wide, send_sums, line_sums, in_sems, send_sems, recv_sems, entered):
    me = lax.axis_index("ctx")
    batch = channels // 2
    fields = 4 * batch
    others = parts - 1
    far = parts // (CORES * across)
    core, z, x = me % CORES, (me // CORES) % across, me // (CORES * across)
    plane = [((x + j) % far) * (CORES * across) + (core + k) % CORES for j in range(far) for k in range(CORES)]
    plane_index = x * CORES + core

    def each_peer(visit):
        def turn(step, carry):
            shift = across // 2 + (1 - 2 * (step % 2)) * ((step + 1) // 2)
            row = ((z + shift) % across) * CORES
            for base in reversed(plane):
                visit(base + row)
            return carry

        lax.fori_loop(0, across - 1, turn, 0)
        for base in reversed(plane[1:]):
            visit(base + z * CORES)

    def push(source, target, n, d):
        pltpu.make_async_remote_copy(source, target, send_sems.at[n], recv_sems.at[n], device_id={"ctx": d}, device_id_type=MESH).start()

    def keep(source, target, n):
        pltpu.make_async_copy(source, target, recv_sems.at[n]).start()

    def wait_bytes(ref, sem):
        pltpu.make_async_copy(ref, ref, sem).wait()

    apart = lax.axis_index("tp") == 0
    last = apart & (me == 0)
    spots = [j * (CORES * across) + k for j in range(far) for k in range(CORES)]
    barrier = pltpu.get_barrier_semaphore()

    def tell(sem, d):
        pl.semaphore_signal(sem, inc=1, device_id={"ctx": d}, device_id_type=MESH)

    def in_rows(d):
        return jnp.logical_not(apart & (d == 0))

    @pl.when(jnp.logical_not(last))
    def _():
        def greet_row(row, carry):
            for spot in spots:
                tell(barrier, spot + row * CORES)
            return carry

        for base in plane[1:]:
            d = base + z * CORES
            pl.when(in_rows(d))(lambda d=d: tell(barrier, d))
        lax.fori_loop(z + 1, across, greet_row, 0)
        pl.when(apart)(lambda: tell(barrier, 0))

    loads = [pltpu.make_async_copy(ref, raw.at[a], in_sems.at[a]) for a, ref in enumerate((q_hbm, k_hbm, v_hbm, g_hbm, h_hbm))]
    pairs = ((taps_hbm, taps_ref), (first_hbm, first_ref), (twist_hbm, twist_ref), (second_hbm, second_ref), (back_hbm, back_ref), (first_back_hbm, first_back_ref))
    tables = [pltpu.make_async_copy(ref, held, in_sems.at[5 + n]) for n, (ref, held) in enumerate(pairs)]
    for copy in loads + tables:
        copy.start()

    for a in (4, 0, 1, 2, 3):
        loads[a].wait()
        columns = raw[a].astype(F32).T
        for c in range(channels):
            block = columns[c * parts : (c + 1) * parts]
            if a < 4:
                wide[c // batch, pl.ds(a * batch + c % batch, parts, stride=fields), :] = block
            else:
                wide_h[pl.ds(c, parts, stride=channels), :] = block
        if a == 4:
            for d in range(parts):
                send_h[d] = wide_h[d * channels : (d + 1) * channels, :].astype(BF16)
    for b in range(2):
        send_a[b] = wide[b].reshape(parts, fields, wide.shape[2]).astype(BF16)
    tables[0].wait()
    lane = lax.broadcasted_iota(jnp.int32, (3, taps_ref.shape[2]), 1)
    for i in range(3):
        taps_i = taps_ref[i].astype(F32)
        for c in range(channels):
            mine = jnp.sum(jnp.where(lane == me + c * parts, taps_i, 0.0), axis=1, keepdims=True)
            tap_rows[c, 3 * i : 3 * i + 3, :] = jnp.broadcast_to(mine, (3, tap_rows.shape[2]))

    known = jnp.where(apart, len(spots) * (z + 1) - 2, len(spots) * (z + 1) - 1)
    pl.semaphore_wait(barrier, jnp.where(last, others, known))

    @pl.when(jnp.logical_not(last))
    def _():
        def tell_row(row, carry):
            for spot in spots[1:]:
                tell(entered.at[z], spot + row * CORES)
            pl.when(in_rows(row * CORES))(lambda: tell(entered.at[z], row * CORES))
            return carry

        lax.fori_loop(0, z, tell_row, 0)

    @pl.when(last)
    def _():
        each_peer(lambda d: tell(entered.at[across], d))

    def each_in_rows(visit, wait):
        def to_row(row, carry):
            if wait:
                pl.when((row > z) & jnp.logical_not(last))(lambda: pl.semaphore_wait(entered.at[row], len(spots)))
            for spot in spots:
                d = spot + row * CORES
                pl.when((d != me) & in_rows(d))(lambda d=d: visit(d))
            return carry

        lax.fori_loop(0, across, to_row, 0)

    def send_first(d):
        push(send_h.at[d], recv_h.at[me], 0, d)
        push(send_a.at[0, d], recv_a.at[0, me], 1, d)

    def send_second(d):
        push(send_a.at[1, d], recv_a.at[1, me], 2, d)

    each_in_rows(send_first, True)
    each_in_rows(send_second, False)

    @pl.when(apart & (me != 0))
    def _():
        pl.semaphore_wait(entered.at[across], 1)
        send_first(0)
        send_second(0)

    keep(send_h.at[me], recv_h.at[me], 0)
    for b in range(2):
        keep(send_a.at[b, me], recv_a.at[b, me], 1 + b)
    for copy in tables[1:]:
        copy.wait()
    sum_rows[...] = jnp.zeros_like(sum_rows)

    def run(b):
        if b == 0:
            wait_bytes(recv_h, recv_sems.at[0])
            for d in range(parts):
                wide_h[d * channels : (d + 1) * channels, :] = recv_h[d].astype(F32)
        wait_bytes(recv_a.at[b], recv_sems.at[1 + b])
        wide[b] = recv_a[b].astype(F32).reshape(parts * fields, wide.shape[2])

        def load(a, c):
            if a < 4:
                return wide[b, pl.ds(a * batch + c, parts, stride=fields), :]
            return wide_h[pl.ds(b * batch + c, parts, stride=channels), :]

        def taps(i, j, c):
            return tap_rows[b * batch + c, 3 * i + j : 3 * i + j + 1, :]

        def store(a, c, value):
            if a < 4:
                wide[b, pl.ds(a * batch + c, parts, stride=fields), :] = value
            else:
                wide_h[pl.ds(b * batch + c, parts, stride=channels), :] = value

        def store_sums(sums):
            for (i, j, c), value in sums:
                at = (i * 3 + j) * channels + b * batch + c
                sum_rows[at : at + 1, :] = value

        layer(load, taps, first_ref[...], twist_ref, second_ref, back_ref, first_back_ref[...], store, store_sums, batch)
        send_out[b] = wide[b].reshape(parts, fields, wide.shape[2]).astype(BF16)

    run(0)
    each_peer(lambda d: push(send_out.at[0, d], got_ref.at[0, me], 3, d))
    keep(send_out.at[0, me], got_ref.at[0, me], 3)
    run(1)
    high, low = halves(sum_rows[...])
    ones = jnp.ones((8, high.shape[1]), BF16)
    along = (((1,), (1,)), ((), ()))
    totals = lax.dot_general(ones, high, along, preferred_element_type=F32) + lax.dot_general(ones, low, along, preferred_element_type=F32)
    send_sums[...] = totals[0:1, :]
    for d in range(parts):
        send_wide[d] = wide_h[d * channels : (d + 1) * channels, :]
    for k in range(1, across):
        push(send_sums, line_sums.at[z], 6, plane[0] + ((z + k) % across) * CORES)
    keep(send_sums, line_sums.at[z], 6)

    def send_last(d):
        push(send_out.at[1, d], got_ref.at[1, me], 4, d)
        push(send_wide.at[d], got_wide_ref.at[me], 5, d)

    each_peer(send_last)
    keep(send_out.at[1, me], got_ref.at[1, me], 4)
    keep(send_wide.at[me], got_wide_ref.at[me], 5)
    wait_bytes(line_sums, recv_sems.at[6])
    for base in plane[1:]:
        push(line_sums, got_sums_ref.at[plane_index], 7, base + z * CORES)
    keep(line_sums, got_sums_ref.at[plane_index], 7)
    for n, ref in enumerate((recv_h, recv_a.at[0], recv_a.at[1], got_ref.at[0], got_ref.at[1], got_wide_ref, line_sums, got_sums_ref)):
        sent = ref.at[pl.ds(0, ref.shape[0] - 1)]
        wait_bytes(sent, send_sems.at[n])
    for n, ref in ((3, got_ref.at[0]), (4, got_ref.at[1]), (5, got_wide_ref), (7, got_sums_ref)):
        wait_bytes(ref, recv_sems.at[n])


def finish_kernel(parts, channels, across, got_ref, got_wide_ref, got_sums_ref, out_hbm, q_hbm, k_hbm, v_hbm, h_hbm, taps_hbm,
                  wide, wide_h, sums, turned, done, done_h, done_taps, sems):
    batch = channels // 2
    fields = 4 * batch
    copies = []

    def put(source, target):
        copies.append(pltpu.make_async_copy(source, target, sems.at[len(copies)]))
        copies[-1].start()

    for d in range(parts):
        wide_h[d * channels : (d + 1) * channels, :] = got_wide_ref[d]
        at = d // (CORES * across) * CORES + d % CORES
        sums[d : d + 1, :] = got_sums_ref[at, (d // CORES) % across]
    blocks = [wide_h[pl.ds(c, parts, stride=channels), :] for c in range(channels)]
    done_h[...] = jnp.concatenate(blocks, axis=0).T
    put(done_h, h_hbm)
    turned[...] = sums[...].T
    rows = jnp.concatenate([turned[pl.ds(c, 9, stride=channels), :] for c in range(channels)], axis=1)
    for i in range(3):
        done_taps[i] = rows[3 * i : 3 * i + 3]
    put(done_taps, taps_hbm)
    for b in range(2):
        wide[b] = got_ref[b].astype(F32).reshape(parts * fields, wide.shape[2])
    for a, ref in enumerate((out_hbm, q_hbm, k_hbm, v_hbm)):
        blocks = [wide[c // batch, pl.ds(a * batch + c % batch, parts, stride=fields), :] for c in range(channels)]
        done[a] = jnp.concatenate(blocks, axis=0).T.astype(BF16)
        put(done.at[a], ref)
    for copy in copies:
        copy.wait()


def local(query_in, key_in, value_in, long_filter, short_taps, out_grad):
    rows, width = query_in.shape
    parts = lax.axis_size("ctx")
    across = 8 if parts == 64 else parts // 4
    channels = width // parts
    fields = 2 * channels
    tables = [jnp.asarray(t) for t in transform_tables(parts, rows)]
    vmem = pl.BlockSpec(memory_space=pltpu.VMEM)
    hbm = pl.BlockSpec(memory_space=pl.ANY)
    planes = parts // across
    both = (2, parts, fields, rows)
    got = pl.pallas_call(
        lambda *refs: exchange_kernel(parts, channels, across, *refs),
        out_shape=(
            pltpu.VMEM(both, BF16),
            pltpu.VMEM((parts, channels, rows), F32),
            pltpu.VMEM((planes, across, 1, rows), F32),
        ),
        in_specs=[hbm] * 11,
        out_specs=(vmem, vmem, vmem),
        scratch_shapes=[pltpu.VMEM((5, rows, width), BF16), pltpu.VMEM(short_taps.shape, BF16)]
        + [pltpu.VMEM(t.shape, t.dtype) for t in tables]
        + [
            pltpu.VMEM((channels, 16, rows), F32),
            pltpu.VMEM((2, parts * fields, rows), F32),
            pltpu.VMEM((parts * channels, rows), F32),
            pltpu.VMEM((rows, rows), F32),
            pltpu.VMEM(both, BF16),
            pltpu.VMEM((parts, channels, rows), BF16),
            pltpu.VMEM(both, BF16),
            pltpu.VMEM((parts, channels, rows), BF16),
            pltpu.VMEM(both, BF16),
            pltpu.VMEM((parts, channels, rows), F32),
            pltpu.VMEM((1, rows), F32),
            pltpu.VMEM((across, 1, rows), F32),
            pltpu.SemaphoreType.DMA((11,)),
            pltpu.SemaphoreType.DMA((8,)),
            pltpu.SemaphoreType.DMA((8,)),
            pltpu.SemaphoreType.REGULAR((across + 1,)),
        ],
        compiler_params=pltpu.CompilerParams(collective_id=0, has_side_effects=True),
        name="exchange_and_layer",
    )(query_in, key_in, value_in, out_grad, long_filter, short_taps, *tables)
    got = [pltpu.with_memory_space_constraint(g, pltpu.VMEM) for g in got]
    field = jax.ShapeDtypeStruct((rows, width), BF16)
    return pl.pallas_call(
        lambda *refs: finish_kernel(parts, channels, across, *refs),
        out_shape=(field, field, field, field, jax.ShapeDtypeStruct((rows, width), F32), jax.ShapeDtypeStruct(short_taps.shape, F32)),
        in_specs=[vmem] * 3,
        out_specs=(hbm,) * 6,
        scratch_shapes=[
            pltpu.VMEM((2, parts * fields, rows), F32),
            pltpu.VMEM((parts * channels, rows), F32),
            pltpu.VMEM((parts, rows), F32),
            pltpu.VMEM((rows, parts), F32),
            pltpu.VMEM((4, rows, width), BF16),
            pltpu.VMEM((rows, width), F32),
            pltpu.VMEM(short_taps.shape, F32),
            pltpu.SemaphoreType.DMA((6,)),
        ],
        name="finish",
    )(*got)


def solution(mesh):
    placed = P("ctx", "tp")
    taps_placed = P(None, None, "tp")
    return jax.shard_map(
        local,
        mesh=mesh,
        in_specs=(placed, placed, placed, placed, taps_placed, placed),
        out_specs=(placed, placed, placed, placed, placed, taps_placed),
        check_vma=False,
    )
```

```python
import math

import jax
import jax.numpy as jnp
import ml_dtypes
import numpy as np
from jax import lax
from jax.experimental import pallas as pl
from jax.experimental.pallas import tpu as pltpu
from jax.sharding import PartitionSpec as P

F32 = jnp.float32
BF16 = jnp.bfloat16


def split_np(table):
    high = table.astype(np.float32).astype(ml_dtypes.bfloat16)
    low = (table - high.astype(np.float64)).astype(np.float32).astype(ml_dtypes.bfloat16)
    return high, low


def transform_tables(blocks, width):
    length = blocks * width
    k1 = np.arange(blocks)[:, None] + 0.25
    s = np.arange(blocks)[None, :]
    p = np.arange(width)[None, :]
    angle = 2.0 * np.pi * k1 * s / blocks
    high, low = split_np(np.concatenate([np.cos(angle), -np.sin(angle)], axis=0))
    first = np.concatenate([high, low, high], axis=1)
    twist_angle = 2.0 * np.pi * k1 * p / length
    twist = np.stack([np.cos(twist_angle), -np.sin(twist_angle)]).astype(np.float32)
    p_col = np.arange(width)[:, None]
    k2 = np.arange(width)[None, :]
    angle2 = 2.0 * np.pi * (p_col * k2 % width) / width
    cosine, sine = np.cos(angle2), np.sin(angle2)
    second = np.stack(split_np(np.block([[cosine, -sine], [sine, cosine]])))
    second_back = np.stack(split_np(np.block([[cosine, sine], [-sine, cosine]])))
    high, low = split_np(np.concatenate([np.cos(angle).T, -np.sin(angle).T], axis=1) / length)
    first_back = np.concatenate([high, low, high], axis=1)
    return first, twist, second, second_back, first_back


def halves(x):
    high = x.astype(BF16)
    low = (x - high.astype(F32)).astype(BF16)
    return high, low


def dot(a, b):
    return jnp.dot(a, b, preferred_element_type=F32)


def later(x, offset, lane, row):
    turned = pltpu.roll(x, offset, 1)
    above = jnp.where(row == 0, 0.0, pltpu.roll(turned, 1, 0))
    return jnp.where(lane < offset, above, turned)


def sooner(x, offset, lane, row):
    rows, width = x.shape
    turned = pltpu.roll(x, width - offset, 1)
    below = jnp.where(row == rows - 1, 0.0, pltpu.roll(turned, rows - 1, 0))
    return jnp.where(lane >= width - offset, below, turned)


def layer(load, taps, first, twist, second, second_back, first_back, store, store_sums, channels):
    width = 128
    rows = twist.shape[1]
    lane = lax.broadcasted_iota(jnp.int32, (rows, width), 1)
    row = lax.broadcasted_iota(jnp.int32, (rows, width), 0)
    shifted = {}
    filtered = {}
    for c in range(channels):
        for i in range(3):
            x = load(i, c)
            shifted[i, c] = [x, later(x, 1, lane, row), later(x, 2, lane, row)]
            filtered[i, c] = sum(taps(i, j, c) * shifted[i, c][j] for j in range(3))
    grads = [load(3, c) for c in range(channels)]
    signals = []
    for c in range(channels):
        signals += [filtered[1, c] * filtered[2, c], grads[c] * filtered[0, c]]
    high, low = halves(jnp.concatenate(signals, axis=1))
    spread = dot(first, jnp.concatenate([high, high, low], axis=0))
    filt = jnp.concatenate([load(4, c) for c in range(channels)], axis=1).astype(BF16)
    spread_filt = dot(first[:, : 2 * rows], jnp.concatenate([filt, filt], axis=0))
    turned = []
    for j in range(3 * channels):
        source, at = (spread, j) if j < 2 * channels else (spread_filt, j - 2 * channels)
        re = source[:rows, at * width : (at + 1) * width]
        im = source[rows:, at * width : (at + 1) * width]
        turned.append(jnp.concatenate([re * twist[0] - im * twist[1], re * twist[1] + im * twist[0]], axis=1))
    high, low = halves(jnp.concatenate(turned, axis=0))
    spectra = dot(high, second[0]) + dot(low, second[0]) + dot(high, second[1])

    def spectrum(j):
        block = spectra[j * rows : (j + 1) * rows]
        return block[:, :width], block[:, width:]

    products = []
    for c in range(channels):
        mr, mi = spectrum(2 * c)
        gr, gi = spectrum(2 * c + 1)
        hr, hi = spectrum(2 * channels + c)
        products.append(jnp.concatenate([mr * hr - mi * hi, mr * hi + mi * hr], axis=1))
        products.append(jnp.concatenate([gr * hr + gi * hi, gi * hr - gr * hi], axis=1))
        products.append(jnp.concatenate([gr * mr + gi * mi, gi * mr - gr * mi], axis=1))
    high, low = halves(jnp.concatenate(products, axis=0))
    back = dot(high, second_back[0]) + dot(low, second_back[0]) + dot(high, second_back[1])
    columns = []
    for j in range(3 * channels):
        re = back[j * rows : (j + 1) * rows, :width]
        im = back[j * rows : (j + 1) * rows, width:]
        columns.append(jnp.concatenate([re * twist[0] + im * twist[1], im * twist[0] - re * twist[1]], axis=0))
    high, low = halves(jnp.concatenate(columns, axis=1))
    result = dot(first_back, jnp.concatenate([high, high, low], axis=0))
    scale = 1.0 / math.sqrt(rows * width)
    sums = []
    for c in range(channels):
        convolved, mixed_grad, filter_grad = (
            result[:, (3 * c + j) * width : (3 * c + j + 1) * width] for j in range(3)
        )
        store(0, c, filtered[0, c] * convolved)
        inner = [grads[c] * convolved, mixed_grad * filtered[2, c], mixed_grad * filtered[1, c]]
        for i in range(3):
            g = inner[i]
            grad = taps(i, 0, c) * g + taps(i, 1, c) * sooner(g, 1, lane, row) + taps(i, 2, c) * sooner(g, 2, lane, row)
            store(1 + i, c, grad)
            for j in range(3):
                sums.append(((i, j, c), jnp.sum(g * shifted[i, c][j], axis=0, keepdims=True) * scale))
        store(4, c, filter_grad * scale)
    store_sums(sums)


MESH = pl.DeviceIdType.MESH
CORES = 2


def exchange_kernel(parts, channels, across, q_hbm, k_hbm, v_hbm, g_hbm, h_hbm, taps_hbm, first_hbm, twist_hbm, second_hbm, back_hbm, first_back_hbm,
                    got_ref, got_wide_ref, got_sums_ref,
                    raw, taps_ref, first_ref, twist_ref, second_ref, back_ref, first_back_ref, tap_rows, wide, wide_h, grad_rows, sum_rows,
                    send_a, send_h, recv_a, recv_h, send_out, send_wide, send_sums, line_sums, in_sems, send_sems, recv_sems, entered):
    me = lax.axis_index("ctx")
    fields = 4
    others = parts - 1
    far = parts // (CORES * across)
    core, z, x = me % CORES, (me // CORES) % across, me // (CORES * across)
    plane = [((x + j) % far) * (CORES * across) + (core + k) % CORES for j in range(far) for k in range(CORES)]
    plane_index = x * CORES + core

    staged = lax.axis_index("tp") % 2 == 0
    apart = lax.axis_index("tp") == 0
    last = apart & (me == 0)

    def each_peer(visit, early_first=False):
        def turn(step, carry):
            shift = across // 2 + (1 - 2 * (step % 2)) * ((step + 1) // 2)
            row = (z + shift) % across
            if early_first:
                row = jnp.where(staged, jnp.where(step < z, step, step + 1), row)
            for base in reversed(plane):
                visit(base + row * CORES)
            return carry

        lax.fori_loop(0, across - 1, turn, 0)
        for base in reversed(plane[1:]):
            visit(base + z * CORES)

    def push(source, target, n, d):
        pltpu.make_async_remote_copy(source, target, send_sems.at[n], recv_sems.at[n], device_id={"ctx": d}, device_id_type=MESH).start()

    def keep(source, target, n):
        pltpu.make_async_copy(source, target, recv_sems.at[n]).start()

    def wait_bytes(ref, sem):
        pltpu.make_async_copy(ref, ref, sem).wait()

    spots = [j * (CORES * across) + k for j in range(far) for k in range(CORES)]
    barrier = pltpu.get_barrier_semaphore()

    def tell(sem, d):
        pl.semaphore_signal(sem, inc=1, device_id={"ctx": d}, device_id_type=MESH)

    def in_rows(d):
        return jnp.logical_not(apart & (d == 0))

    @pl.when(jnp.logical_not(staged))
    def _():
        each_peer(lambda d: tell(barrier, d))

    @pl.when(staged & jnp.logical_not(last))
    def _():
        def greet_row(row, carry):
            for spot in spots:
                tell(barrier, spot + row * CORES)
            return carry

        for base in plane[1:]:
            d = base + z * CORES
            pl.when(in_rows(d))(lambda d=d: tell(barrier, d))
        lax.fori_loop(z + 1, across, greet_row, 0)
        pl.when(apart)(lambda: tell(barrier, 0))

    loads = [pltpu.make_async_copy(ref, raw.at[a], in_sems.at[a]) for a, ref in enumerate((q_hbm, k_hbm, v_hbm, g_hbm, h_hbm))]
    pairs = ((taps_hbm, taps_ref), (first_hbm, first_ref), (twist_hbm, twist_ref), (second_hbm, second_ref), (back_hbm, back_ref), (first_back_hbm, first_back_ref))
    tables = [pltpu.make_async_copy(ref, held, in_sems.at[5 + n]) for n, (ref, held) in enumerate(pairs)]
    for copy in loads + tables:
        copy.start()

    known = jnp.where(apart, len(spots) * (z + 1) - 2, len(spots) * (z + 1) - 1)
    pl.semaphore_wait(barrier, jnp.where(last | jnp.logical_not(staged), others, known))

    @pl.when(staged & jnp.logical_not(last))
    def _():
        def tell_row(row, carry):
            for spot in spots[1:]:
                tell(entered.at[z], spot + row * CORES)
            pl.when(in_rows(row * CORES))(lambda: tell(entered.at[z], row * CORES))
            return carry

        lax.fori_loop(0, z, tell_row, 0)

    @pl.when(last)
    def _():
        each_peer(lambda d: tell(entered.at[across], d))

    for a in (4, 0, 1, 2, 3):
        loads[a].wait()
        columns = raw[a].astype(F32).T
        for c in range(channels):
            block = columns[c * parts : (c + 1) * parts]
            if a < 4:
                wide[c, pl.ds(a, parts, stride=fields), :] = block
            else:
                wide_h[c // 2, pl.ds(c % 2, parts, stride=2), :] = block
        if a == 4:
            for b in range(2):
                for d in range(parts):
                    send_h[b, d] = wide_h[b, 2 * d : 2 * d + 2, :].astype(BF16)
    for c in range(channels):
        for d in range(parts):
            send_a[c, d] = wide[c, d * fields : (d + 1) * fields, :].astype(BF16)
    tables[0].wait()
    lane = lax.broadcasted_iota(jnp.int32, (3, taps_ref.shape[2]), 1)
    for i in range(3):
        taps_i = taps_ref[i].astype(F32)
        for c in range(channels):
            mine = jnp.sum(jnp.where(lane == me + c * parts, taps_i, 0.0), axis=1, keepdims=True)
            tap_rows[c, 3 * i : 3 * i + 3, :] = jnp.broadcast_to(mine, (3, tap_rows.shape[2]))

    def to_row(visit, row):
        for spot in spots:
            d = spot + row * CORES
            pl.when((d != me) & in_rows(d))(lambda d=d: visit(d))

    def send_chunk(c, d, pair=None):
        if pair is not None:
            push(send_h.at[pair, d], recv_h.at[pair, me], 4 + pair, d)
        push(send_a.at[c, d], recv_a.at[c, me], c, d)

    sends = [lambda d: send_chunk(0, d, 0), lambda d: send_chunk(1, d), lambda d: send_chunk(2, d, 1), lambda d: send_chunk(3, d)]

    def to_rows(visit):
        def step(row, carry):
            to_row(visit, row)
            return carry

        return step

    def next_row(row, carry):
        to_row(sends[1], row - 1)
        pl.semaphore_wait(entered.at[row], len(spots))
        to_row(sends[0], row)
        return carry

    @pl.when(staged)
    def _():
        inside = jnp.where(last, across - 1, z)
        lax.fori_loop(0, inside + 1, to_rows(sends[0]), 0)
        lax.fori_loop(0, inside, to_rows(sends[1]), 0)
        lax.fori_loop(inside + 1, across, next_row, 0)
        to_row(sends[1], across - 1)
        lax.fori_loop(0, across, to_rows(sends[2]), 0)
        lax.fori_loop(0, across, to_rows(sends[3]), 0)

    @pl.when(jnp.logical_not(staged))
    def _():
        for visit in sends:
            each_peer(visit)

    @pl.when(apart & (me != 0))
    def _():
        pl.semaphore_wait(entered.at[across], 1)
        for visit in sends:
            visit(0)

    for b in range(2):
        keep(send_h.at[b, me], recv_h.at[b, me], 4 + b)
    for c in range(channels):
        keep(send_a.at[c, me], recv_a.at[c, me], c)
    for copy in tables[1:]:
        copy.wait()
    sum_rows[...] = jnp.zeros_like(sum_rows)

    def run(c, carry):
        @pl.when(c % 2 == 0)
        def _():
            wait_bytes(recv_h.at[c // 2], recv_sems.at[4 + c // 2])
            for d in range(parts):
                wide_h[c // 2, 2 * d : 2 * d + 2, :] = recv_h[c // 2, d].astype(F32)

        wait_bytes(recv_a.at[c], recv_sems.at[c])
        for d in range(parts):
            wide[c, d * fields : (d + 1) * fields, :] = recv_a[c, d].astype(F32)

        def load(a, _):
            if a < 4:
                return wide[c, pl.ds(a, parts, stride=fields), :]
            return wide_h[c // 2, pl.ds(c % 2, parts, stride=2), :]

        def taps(i, j, _):
            return tap_rows[c, 3 * i + j : 3 * i + j + 1, :]

        def store(a, _, value):
            if a < 4:
                wide[c, pl.ds(a, parts, stride=fields), :] = value
            else:
                grad_rows[c] = value

        def store_sums(sums):
            for (i, j, _), value in sums:
                sum_rows[c, 3 * i + j : 3 * i + j + 1, :] = value

        layer(load, taps, first_ref[...], twist_ref, second_ref, back_ref, first_back_ref[...], store, store_sums, 1)
        for d in range(parts):
            send_out[c, d] = wide[c, d * fields : (d + 1) * fields, :].astype(BF16)
            send_wide[c, d] = grad_rows[c, d : d + 1, :]

        def send_back(d):
            push(send_out.at[c, d], got_ref.at[c, me], 6 + c, d)
            push(send_wide.at[c, d], got_wide_ref.at[c, me], 10 + c, d)

        @pl.when(c == channels - 1)
        def _():
            high, low = halves(sum_rows[...].reshape(channels * 16, sum_rows.shape[2]))
            high = jnp.concatenate([high, jnp.zeros_like(high)], axis=0)
            low = jnp.concatenate([low, jnp.zeros_like(low)], axis=0)
            ones = jnp.ones((8, high.shape[1]), BF16)
            along = (((1,), (1,)), ((), ()))
            totals = lax.dot_general(ones, high, along, preferred_element_type=F32) + lax.dot_general(ones, low, along, preferred_element_type=F32)
            send_sums[...] = totals[0:1, :]
            for k in range(1, across):
                push(send_sums, line_sums.at[z], 14, plane[0] + ((z + k) % across) * CORES)
            keep(send_sums, line_sums.at[z], 14)

        each_peer(send_back, True)
        keep(send_out.at[c, me], got_ref.at[c, me], 6 + c)
        keep(send_wide.at[c, me], got_wide_ref.at[c, me], 10 + c)
        return carry

    lax.fori_loop(0, channels, run, 0)
    wait_bytes(line_sums, recv_sems.at[14])
    for base in plane[1:]:
        push(line_sums, got_sums_ref.at[plane_index], 15, base + z * CORES)
    keep(line_sums, got_sums_ref.at[plane_index], 15)
    sent = [recv_a.at[c] for c in range(channels)] + [recv_h.at[b] for b in range(2)]
    sent += [got_ref.at[c] for c in range(channels)] + [got_wide_ref.at[c] for c in range(channels)] + [line_sums, got_sums_ref]
    for n, ref in enumerate(sent):
        wait_bytes(ref.at[pl.ds(0, ref.shape[0] - 1)], send_sems.at[n])
    for n in (*range(6, 14), 15):
        wait_bytes(sent[n], recv_sems.at[n])


def finish_kernel(parts, channels, across, got_ref, got_wide_ref, got_sums_ref, out_hbm, q_hbm, k_hbm, v_hbm, h_hbm, taps_hbm,
                  wide, wide_h, sums, turned, done, done_h, done_taps, sems):
    fields = 4
    copies = []

    def put(source, target):
        copies.append(pltpu.make_async_copy(source, target, sems.at[len(copies)]))
        copies[-1].start()

    for d in range(parts):
        for c in range(channels):
            wide_h[c * parts + d : c * parts + d + 1, :] = got_wide_ref[c, d]
        at = d // (CORES * across) * CORES + d % CORES
        sums[d : d + 1, :] = got_sums_ref[at, (d // CORES) % across]
    done_h[...] = wide_h[...].T
    put(done_h, h_hbm)
    turned[...] = sums[...].T
    rows = jnp.concatenate([turned[16 * c : 16 * c + 9, :] for c in range(channels)], axis=1)
    for i in range(3):
        done_taps[i] = rows[3 * i : 3 * i + 3]
    put(done_taps, taps_hbm)
    for c in range(channels):
        for d in range(parts):
            wide[c, d * fields : (d + 1) * fields, :] = got_ref[c, d].astype(F32)
    for a, ref in enumerate((out_hbm, q_hbm, k_hbm, v_hbm)):
        blocks = [wide[c, pl.ds(a, parts, stride=fields), :] for c in range(channels)]
        done[a] = jnp.concatenate(blocks, axis=0).T.astype(BF16)
        put(done.at[a], ref)
    for copy in copies:
        copy.wait()


def local(query_in, key_in, value_in, long_filter, short_taps, out_grad):
    rows, width = query_in.shape
    parts = lax.axis_size("ctx")
    across = 8 if parts == 64 else parts // 4
    channels = width // parts
    fields = 4
    tables = [jnp.asarray(t) for t in transform_tables(parts, rows)]
    vmem = pl.BlockSpec(memory_space=pltpu.VMEM)
    hbm = pl.BlockSpec(memory_space=pl.ANY)
    planes = parts // across
    chunks = (channels, parts, fields, rows)
    pairs = (2, parts, 2, rows)
    got = pl.pallas_call(
        lambda *refs: exchange_kernel(parts, channels, across, *refs),
        out_shape=(
            pltpu.VMEM(chunks, BF16),
            pltpu.VMEM((channels, parts, 1, rows), F32),
            pltpu.VMEM((planes, across, 1, rows), F32),
        ),
        in_specs=[hbm] * 11,
        out_specs=(vmem, vmem, vmem),
        scratch_shapes=[pltpu.VMEM((5, rows, width), BF16), pltpu.VMEM(short_taps.shape, BF16)]
        + [pltpu.VMEM(t.shape, t.dtype) for t in tables]
        + [
            pltpu.VMEM((channels, 16, rows), F32),
            pltpu.VMEM((channels, parts * fields, rows), F32),
            pltpu.VMEM((2, parts * 2, rows), F32),
            pltpu.VMEM((channels, parts, rows), F32),
            pltpu.VMEM((channels, 16, rows), F32),
            pltpu.VMEM(chunks, BF16),
            pltpu.VMEM(pairs, BF16),
            pltpu.VMEM(chunks, BF16),
            pltpu.VMEM(pairs, BF16),
            pltpu.VMEM(chunks, BF16),
            pltpu.VMEM((channels, parts, 1, rows), F32),
            pltpu.VMEM((1, rows), F32),
            pltpu.VMEM((across, 1, rows), F32),
            pltpu.SemaphoreType.DMA((11,)),
            pltpu.SemaphoreType.DMA((16,)),
            pltpu.SemaphoreType.DMA((16,)),
            pltpu.SemaphoreType.REGULAR((across + 1,)),
        ],
        compiler_params=pltpu.CompilerParams(collective_id=0, has_side_effects=True),
        name="exchange_and_layer",
    )(query_in, key_in, value_in, out_grad, long_filter, short_taps, *tables)
    got = [pltpu.with_memory_space_constraint(g, pltpu.VMEM) for g in got]
    field = jax.ShapeDtypeStruct((rows, width), BF16)
    return pl.pallas_call(
        lambda *refs: finish_kernel(parts, channels, across, *refs),
        out_shape=(field, field, field, field, jax.ShapeDtypeStruct((rows, width), F32), jax.ShapeDtypeStruct(short_taps.shape, F32)),
        in_specs=[vmem] * 3,
        out_specs=(hbm,) * 6,
        scratch_shapes=[
            pltpu.VMEM((channels, parts * fields, rows), F32),
            pltpu.VMEM((parts * channels, rows), F32),
            pltpu.VMEM((parts, rows), F32),
            pltpu.VMEM((rows, parts), F32),
            pltpu.VMEM((4, rows, width), BF16),
            pltpu.VMEM((rows, width), F32),
            pltpu.VMEM(short_taps.shape, F32),
            pltpu.SemaphoreType.DMA((6,)),
        ],
        name="finish",
    )(*got)


def solution(mesh):
    placed = P("ctx", "tp")
    taps_placed = P(None, None, "tp")
    return jax.shard_map(
        local,
        mesh=mesh,
        in_specs=(placed, placed, placed, placed, taps_placed, placed),
        out_specs=(placed, placed, placed, placed, placed, taps_placed),
        check_vma=False,
    )
```

```python
import math

import jax
import jax.numpy as jnp
import ml_dtypes
import numpy as np
from jax import lax
from jax.experimental import pallas as pl
from jax.experimental.pallas import tpu as pltpu
from jax.sharding import PartitionSpec as P

F32 = jnp.float32
BF16 = jnp.bfloat16


def split_np(table):
    high = table.astype(np.float32).astype(ml_dtypes.bfloat16)
    low = (table - high.astype(np.float64)).astype(np.float32).astype(ml_dtypes.bfloat16)
    return high, low


def transform_tables(blocks, width):
    length = blocks * width
    k1 = np.arange(blocks)[:, None] + 0.25
    s = np.arange(blocks)[None, :]
    p = np.arange(width)[None, :]
    angle = 2.0 * np.pi * k1 * s / blocks
    high, low = split_np(np.concatenate([np.cos(angle), -np.sin(angle)], axis=0))
    first = np.concatenate([high, low, high], axis=1)
    twist_angle = 2.0 * np.pi * k1 * p / length
    twist = np.stack([np.cos(twist_angle), -np.sin(twist_angle)]).astype(np.float32)
    p_col = np.arange(width)[:, None]
    k2 = np.arange(width)[None, :]
    angle2 = 2.0 * np.pi * (p_col * k2 % width) / width
    cosine, sine = np.cos(angle2), np.sin(angle2)
    second = np.stack(split_np(np.block([[cosine, -sine], [sine, cosine]])))
    second_back = np.stack(split_np(np.block([[cosine, sine], [-sine, cosine]])))
    high, low = split_np(np.concatenate([np.cos(angle).T, -np.sin(angle).T], axis=1) / length)
    first_back = np.concatenate([high, low, high], axis=1)
    return first, twist, second, second_back, first_back


def halves(x):
    high = x.astype(BF16)
    low = (x - high.astype(F32)).astype(BF16)
    return high, low


def dot(a, b):
    return jnp.dot(a, b, preferred_element_type=F32)


def later(x, offset, lane, row):
    turned = pltpu.roll(x, offset, 1)
    above = jnp.where(row == 0, 0.0, pltpu.roll(turned, 1, 0))
    return jnp.where(lane < offset, above, turned)


def sooner(x, offset, lane, row):
    rows, width = x.shape
    turned = pltpu.roll(x, width - offset, 1)
    below = jnp.where(row == rows - 1, 0.0, pltpu.roll(turned, rows - 1, 0))
    return jnp.where(lane >= width - offset, below, turned)


def layer(load, taps, first, twist, second, second_back, first_back, store, store_sums, channels):
    width = 128
    rows = twist.shape[1]
    lane = lax.broadcasted_iota(jnp.int32, (rows, width), 1)
    row = lax.broadcasted_iota(jnp.int32, (rows, width), 0)
    shifted = {}
    filtered = {}
    for c in range(channels):
        for i in range(3):
            x = load(i, c)
            shifted[i, c] = [x, later(x, 1, lane, row), later(x, 2, lane, row)]
            filtered[i, c] = sum(taps(i, j, c) * shifted[i, c][j] for j in range(3))
    grads = [load(3, c) for c in range(channels)]
    signals = []
    for c in range(channels):
        signals += [filtered[1, c] * filtered[2, c], grads[c] * filtered[0, c]]
    high, low = halves(jnp.concatenate(signals, axis=1))
    spread = dot(first, jnp.concatenate([high, high, low], axis=0))
    filt = jnp.concatenate([load(4, c) for c in range(channels)], axis=1).astype(BF16)
    spread_filt = dot(first[:, : 2 * rows], jnp.concatenate([filt, filt], axis=0))
    turned = []
    for j in range(3 * channels):
        source, at = (spread, j) if j < 2 * channels else (spread_filt, j - 2 * channels)
        re = source[:rows, at * width : (at + 1) * width]
        im = source[rows:, at * width : (at + 1) * width]
        turned.append(jnp.concatenate([re * twist[0] - im * twist[1], re * twist[1] + im * twist[0]], axis=1))
    high, low = halves(jnp.concatenate(turned, axis=0))
    spectra = dot(high, second[0]) + dot(low, second[0]) + dot(high, second[1])

    def spectrum(j):
        block = spectra[j * rows : (j + 1) * rows]
        return block[:, :width], block[:, width:]

    products = []
    for c in range(channels):
        mr, mi = spectrum(2 * c)
        gr, gi = spectrum(2 * c + 1)
        hr, hi = spectrum(2 * channels + c)
        products.append(jnp.concatenate([mr * hr - mi * hi, mr * hi + mi * hr], axis=1))
        products.append(jnp.concatenate([gr * hr + gi * hi, gi * hr - gr * hi], axis=1))
        products.append(jnp.concatenate([gr * mr + gi * mi, gi * mr - gr * mi], axis=1))
    high, low = halves(jnp.concatenate(products, axis=0))
    back = dot(high, second_back[0]) + dot(low, second_back[0]) + dot(high, second_back[1])
    columns = []
    for j in range(3 * channels):
        re = back[j * rows : (j + 1) * rows, :width]
        im = back[j * rows : (j + 1) * rows, width:]
        columns.append(jnp.concatenate([re * twist[0] + im * twist[1], im * twist[0] - re * twist[1]], axis=0))
    high, low = halves(jnp.concatenate(columns, axis=1))
    result = dot(first_back, jnp.concatenate([high, high, low], axis=0))
    scale = 1.0 / math.sqrt(rows * width)
    sums = []
    for c in range(channels):
        convolved, mixed_grad, filter_grad = (
            result[:, (3 * c + j) * width : (3 * c + j + 1) * width] for j in range(3)
        )
        store(0, c, filtered[0, c] * convolved)
        inner = [grads[c] * convolved, mixed_grad * filtered[2, c], mixed_grad * filtered[1, c]]
        for i in range(3):
            g = inner[i]
            grad = taps(i, 0, c) * g + taps(i, 1, c) * sooner(g, 1, lane, row) + taps(i, 2, c) * sooner(g, 2, lane, row)
            store(1 + i, c, grad)
            for j in range(3):
                sums.append(((i, j, c), jnp.sum(g * shifted[i, c][j], axis=0, keepdims=True) * scale))
        store(4, c, filter_grad * scale)
    store_sums(sums)


MESH = pl.DeviceIdType.MESH
CORES = 2


def exchange_kernel(parts, channels, across, q_hbm, k_hbm, v_hbm, g_hbm, h_hbm, taps_hbm, first_hbm, twist_hbm, second_hbm, back_hbm, first_back_hbm,
                    got_ref, got_wide_ref, got_sums_ref,
                    raw, taps_ref, first_ref, twist_ref, second_ref, back_ref, first_back_ref, tap_rows, wide, wide_h, sum_rows,
                    send_a, send_h, recv_a, recv_h, send_out, send_wide, send_sums, line_sums, in_sems, send_sems, recv_sems):
    me = lax.axis_index("ctx")
    batch = channels // 2
    fields = 4 * batch
    others = parts - 1
    far = parts // (CORES * across)
    core, z, x = me % CORES, (me // CORES) % across, me // (CORES * across)
    plane = [((x + j) % far) * (CORES * across) + (core + k) % CORES for j in range(far) for k in range(CORES)]
    plane_index = x * CORES + core

    skewed = lax.axis_index("tp") % 2 == 0

    def each_peer(visit, early_first=False):
        def turn(step, carry):
            shift = across // 2 + (1 - 2 * (step % 2)) * ((step + 1) // 2)
            row = (z + shift) % across
            if early_first:
                row = jnp.where(skewed, jnp.where(step < z, step, step + 1), row)
            for base in reversed(plane):
                visit(base + row * CORES)
            return carry

        lax.fori_loop(0, across - 1, turn, 0)
        for base in reversed(plane[1:]):
            visit(base + z * CORES)

    def push(source, target, n, d):
        pltpu.make_async_remote_copy(source, target, send_sems.at[n], recv_sems.at[n], device_id={"ctx": d}, device_id_type=MESH).start()

    def keep(source, target, n):
        pltpu.make_async_copy(source, target, recv_sems.at[n]).start()

    def wait_bytes(ref, sem):
        pltpu.make_async_copy(ref, ref, sem).wait()

    barrier = pltpu.get_barrier_semaphore()
    each_peer(lambda d: pl.semaphore_signal(barrier, inc=1, device_id={"ctx": d}, device_id_type=MESH))
    loads = [pltpu.make_async_copy(ref, raw.at[a], in_sems.at[a]) for a, ref in enumerate((q_hbm, k_hbm, v_hbm, g_hbm, h_hbm))]
    pairs = ((taps_hbm, taps_ref), (first_hbm, first_ref), (twist_hbm, twist_ref), (second_hbm, second_ref), (back_hbm, back_ref), (first_back_hbm, first_back_ref))
    tables = [pltpu.make_async_copy(ref, held, in_sems.at[5 + n]) for n, (ref, held) in enumerate(pairs)]
    for copy in loads + tables:
        copy.start()

    for a in (4, 0, 1, 2, 3):
        loads[a].wait()
        columns = raw[a].astype(F32).T
        for c in range(channels):
            block = columns[c * parts : (c + 1) * parts]
            if a < 4:
                wide[c // batch, pl.ds(a * batch + c % batch, parts, stride=fields), :] = block
            else:
                wide_h[pl.ds(c, parts, stride=channels), :] = block
        if a == 4:
            for d in range(parts):
                send_h[d] = wide_h[d * channels : (d + 1) * channels, :].astype(BF16)
    for b in range(2):
        send_a[b] = wide[b].reshape(parts, fields, wide.shape[2]).astype(BF16)
    tables[0].wait()
    lane = lax.broadcasted_iota(jnp.int32, (3, taps_ref.shape[2]), 1)
    for i in range(3):
        taps_i = taps_ref[i].astype(F32)
        for c in range(channels):
            mine = jnp.sum(jnp.where(lane == me + c * parts, taps_i, 0.0), axis=1, keepdims=True)
            tap_rows[c, 3 * i : 3 * i + 3, :] = jnp.broadcast_to(mine, (3, tap_rows.shape[2]))

    pl.semaphore_wait(barrier, others)

    def send_first(d):
        push(send_h.at[d], recv_h.at[me], 0, d)
        push(send_a.at[0, d], recv_a.at[0, me], 1, d)

    each_peer(send_first)
    each_peer(lambda d: push(send_a.at[1, d], recv_a.at[1, me], 2, d))
    keep(send_h.at[me], recv_h.at[me], 0)
    for b in range(2):
        keep(send_a.at[b, me], recv_a.at[b, me], 1 + b)
    for copy in tables[1:]:
        copy.wait()
    sum_rows[...] = jnp.zeros_like(sum_rows)

    def run(b):
        if b == 0:
            wait_bytes(recv_h, recv_sems.at[0])
            for d in range(parts):
                wide_h[d * channels : (d + 1) * channels, :] = recv_h[d].astype(F32)
        wait_bytes(recv_a.at[b], recv_sems.at[1 + b])
        wide[b] = recv_a[b].astype(F32).reshape(parts * fields, wide.shape[2])

        def load(a, c):
            if a < 4:
                return wide[b, pl.ds(a * batch + c, parts, stride=fields), :]
            return wide_h[pl.ds(b * batch + c, parts, stride=channels), :]

        def taps(i, j, c):
            return tap_rows[b * batch + c, 3 * i + j : 3 * i + j + 1, :]

        def store(a, c, value):
            if a < 4:
                wide[b, pl.ds(a * batch + c, parts, stride=fields), :] = value
            else:
                wide_h[pl.ds(b * batch + c, parts, stride=channels), :] = value

        def store_sums(sums):
            for (i, j, c), value in sums:
                at = (i * 3 + j) * channels + b * batch + c
                sum_rows[at : at + 1, :] = value

        layer(load, taps, first_ref[...], twist_ref, second_ref, back_ref, first_back_ref[...], store, store_sums, batch)
        send_out[b] = wide[b].reshape(parts, fields, wide.shape[2]).astype(BF16)
        for d in range(parts):
            send_wide[b, d] = wide_h[d * channels + b * batch : d * channels + (b + 1) * batch, :]

    def send_back(b):
        def visit(d):
            push(send_out.at[b, d], got_ref.at[b, me], 3 + b, d)
            push(send_wide.at[b, d], got_wide_ref.at[b, me], 5 + b, d)

        each_peer(visit, True)
        keep(send_out.at[b, me], got_ref.at[b, me], 3 + b)
        keep(send_wide.at[b, me], got_wide_ref.at[b, me], 5 + b)

    run(0)
    send_back(0)
    run(1)
    high, low = halves(sum_rows[...])
    ones = jnp.ones((8, high.shape[1]), BF16)
    along = (((1,), (1,)), ((), ()))
    totals = lax.dot_general(ones, high, along, preferred_element_type=F32) + lax.dot_general(ones, low, along, preferred_element_type=F32)
    send_sums[...] = totals[0:1, :]
    for k in range(1, across):
        push(send_sums, line_sums.at[z], 7, plane[0] + ((z + k) % across) * CORES)
    keep(send_sums, line_sums.at[z], 7)
    send_back(1)
    wait_bytes(line_sums, recv_sems.at[7])
    for base in plane[1:]:
        push(line_sums, got_sums_ref.at[plane_index], 8, base + z * CORES)
    keep(line_sums, got_sums_ref.at[plane_index], 8)
    for n, ref in enumerate((recv_h, recv_a.at[0], recv_a.at[1], got_ref.at[0], got_ref.at[1], got_wide_ref.at[0], got_wide_ref.at[1], line_sums, got_sums_ref)):
        sent = ref.at[pl.ds(0, ref.shape[0] - 1)]
        wait_bytes(sent, send_sems.at[n])
    for n, ref in ((3, got_ref.at[0]), (4, got_ref.at[1]), (5, got_wide_ref.at[0]), (6, got_wide_ref.at[1]), (8, got_sums_ref)):
        wait_bytes(ref, recv_sems.at[n])


def finish_kernel(parts, channels, across, got_ref, got_wide_ref, got_sums_ref, out_hbm, q_hbm, k_hbm, v_hbm, h_hbm, taps_hbm,
                  wide, wide_h, sums, turned, done, done_h, done_taps, sems):
    batch = channels // 2
    fields = 4 * batch
    copies = []

    def put(source, target):
        copies.append(pltpu.make_async_copy(source, target, sems.at[len(copies)]))
        copies[-1].start()

    for d in range(parts):
        for b in range(2):
            wide_h[d * channels + b * batch : d * channels + (b + 1) * batch, :] = got_wide_ref[b, d]
        at = d // (CORES * across) * CORES + d % CORES
        sums[d : d + 1, :] = got_sums_ref[at, (d // CORES) % across]
    blocks = [wide_h[pl.ds(c, parts, stride=channels), :] for c in range(channels)]
    done_h[...] = jnp.concatenate(blocks, axis=0).T
    put(done_h, h_hbm)
    turned[...] = sums[...].T
    rows = jnp.concatenate([turned[pl.ds(c, 9, stride=channels), :] for c in range(channels)], axis=1)
    for i in range(3):
        done_taps[i] = rows[3 * i : 3 * i + 3]
    put(done_taps, taps_hbm)
    for b in range(2):
        wide[b] = got_ref[b].astype(F32).reshape(parts * fields, wide.shape[2])
    for a, ref in enumerate((out_hbm, q_hbm, k_hbm, v_hbm)):
        blocks = [wide[c // batch, pl.ds(a * batch + c % batch, parts, stride=fields), :] for c in range(channels)]
        done[a] = jnp.concatenate(blocks, axis=0).T.astype(BF16)
        put(done.at[a], ref)
    for copy in copies:
        copy.wait()


def local(query_in, key_in, value_in, long_filter, short_taps, out_grad):
    rows, width = query_in.shape
    parts = lax.axis_size("ctx")
    across = 8 if parts == 64 else parts // 4
    channels = width // parts
    fields = 2 * channels
    tables = [jnp.asarray(t) for t in transform_tables(parts, rows)]
    vmem = pl.BlockSpec(memory_space=pltpu.VMEM)
    hbm = pl.BlockSpec(memory_space=pl.ANY)
    planes = parts // across
    both = (2, parts, fields, rows)
    got = pl.pallas_call(
        lambda *refs: exchange_kernel(parts, channels, across, *refs),
        out_shape=(
            pltpu.VMEM(both, BF16),
            pltpu.VMEM((2, parts, 2, rows), F32),
            pltpu.VMEM((planes, across, 1, rows), F32),
        ),
        in_specs=[hbm] * 11,
        out_specs=(vmem, vmem, vmem),
        scratch_shapes=[pltpu.VMEM((5, rows, width), BF16), pltpu.VMEM(short_taps.shape, BF16)]
        + [pltpu.VMEM(t.shape, t.dtype) for t in tables]
        + [
            pltpu.VMEM((channels, 16, rows), F32),
            pltpu.VMEM((2, parts * fields, rows), F32),
            pltpu.VMEM((parts * channels, rows), F32),
            pltpu.VMEM((rows, rows), F32),
            pltpu.VMEM(both, BF16),
            pltpu.VMEM((parts, channels, rows), BF16),
            pltpu.VMEM(both, BF16),
            pltpu.VMEM((parts, channels, rows), BF16),
            pltpu.VMEM(both, BF16),
            pltpu.VMEM((2, parts, 2, rows), F32),
            pltpu.VMEM((1, rows), F32),
            pltpu.VMEM((across, 1, rows), F32),
            pltpu.SemaphoreType.DMA((11,)),
            pltpu.SemaphoreType.DMA((9,)),
            pltpu.SemaphoreType.DMA((9,)),
        ],
        compiler_params=pltpu.CompilerParams(collective_id=0, has_side_effects=True),
        name="exchange_and_layer",
    )(query_in, key_in, value_in, out_grad, long_filter, short_taps, *tables)
    got = [pltpu.with_memory_space_constraint(g, pltpu.VMEM) for g in got]
    field = jax.ShapeDtypeStruct((rows, width), BF16)
    return pl.pallas_call(
        lambda *refs: finish_kernel(parts, channels, across, *refs),
        out_shape=(field, field, field, field, jax.ShapeDtypeStruct((rows, width), F32), jax.ShapeDtypeStruct(short_taps.shape, F32)),
        in_specs=[vmem] * 3,
        out_specs=(hbm,) * 6,
        scratch_shapes=[
            pltpu.VMEM((2, parts * fields, rows), F32),
            pltpu.VMEM((parts * channels, rows), F32),
            pltpu.VMEM((parts, rows), F32),
            pltpu.VMEM((rows, parts), F32),
            pltpu.VMEM((4, rows, width), BF16),
            pltpu.VMEM((rows, width), F32),
            pltpu.VMEM(short_taps.shape, F32),
            pltpu.SemaphoreType.DMA((6,)),
        ],
        name="finish",
    )(*got)


def solution(mesh):
    placed = P("ctx", "tp")
    taps_placed = P(None, None, "tp")
    return jax.shard_map(
        local,
        mesh=mesh,
        in_specs=(placed, placed, placed, placed, taps_placed, placed),
        out_specs=(placed, placed, placed, placed, placed, taps_placed),
        check_vma=False,
    )
```

```python
import math

import jax
import jax.numpy as jnp
import ml_dtypes
import numpy as np
from jax import lax
from jax.experimental import pallas as pl
from jax.experimental.pallas import tpu as pltpu
from jax.sharding import PartitionSpec as P

F32 = jnp.float32
BF16 = jnp.bfloat16


def split_np(table):
    high = table.astype(np.float32).astype(ml_dtypes.bfloat16)
    low = (table - high.astype(np.float64)).astype(np.float32).astype(ml_dtypes.bfloat16)
    return high, low


def transform_tables(blocks, width):
    length = blocks * width
    k1 = np.arange(blocks)[:, None] + 0.25
    s = np.arange(blocks)[None, :]
    p = np.arange(width)[None, :]
    angle = 2.0 * np.pi * k1 * s / blocks
    high, low = split_np(np.concatenate([np.cos(angle), -np.sin(angle)], axis=0))
    first = np.concatenate([high, low, high], axis=1)
    twist_angle = 2.0 * np.pi * k1 * p / length
    twist = np.stack([np.cos(twist_angle), -np.sin(twist_angle)]).astype(np.float32)
    p_col = np.arange(width)[:, None]
    k2 = np.arange(width)[None, :]
    angle2 = 2.0 * np.pi * (p_col * k2 % width) / width
    cosine, sine = np.cos(angle2), np.sin(angle2)
    second = np.stack(split_np(np.block([[cosine, -sine], [sine, cosine]])))
    second_back = np.stack(split_np(np.block([[cosine, sine], [-sine, cosine]])))
    high, low = split_np(np.concatenate([np.cos(angle).T, -np.sin(angle).T], axis=1) / length)
    first_back = np.concatenate([high, low, high], axis=1)
    return first, twist, second, second_back, first_back


def halves(x):
    high = x.astype(BF16)
    low = (x - high.astype(F32)).astype(BF16)
    return high, low


def dot(a, b):
    return jnp.dot(a, b, preferred_element_type=F32)


def later(x, offset, lane, row):
    turned = pltpu.roll(x, offset, 1)
    above = jnp.where(row == 0, 0.0, pltpu.roll(turned, 1, 0))
    return jnp.where(lane < offset, above, turned)


def sooner(x, offset, lane, row):
    rows, width = x.shape
    turned = pltpu.roll(x, width - offset, 1)
    below = jnp.where(row == rows - 1, 0.0, pltpu.roll(turned, rows - 1, 0))
    return jnp.where(lane >= width - offset, below, turned)


def layer(load, taps, first, twist, second, second_back, first_back, store, store_sums, channels):
    width = 128
    rows = twist.shape[1]
    lane = lax.broadcasted_iota(jnp.int32, (rows, width), 1)
    row = lax.broadcasted_iota(jnp.int32, (rows, width), 0)
    shifted = {}
    filtered = {}
    for c in range(channels):
        for i in range(3):
            x = load(i, c)
            shifted[i, c] = [x, later(x, 1, lane, row), later(x, 2, lane, row)]
            filtered[i, c] = sum(taps(i, j, c) * shifted[i, c][j] for j in range(3))
    grads = [load(3, c) for c in range(channels)]
    signals = []
    for c in range(channels):
        signals += [filtered[1, c] * filtered[2, c], grads[c] * filtered[0, c]]
    high, low = halves(jnp.concatenate(signals, axis=1))
    spread = dot(first, jnp.concatenate([high, high, low], axis=0))
    filt = jnp.concatenate([load(4, c) for c in range(channels)], axis=1).astype(BF16)
    spread_filt = dot(first[:, : 2 * rows], jnp.concatenate([filt, filt], axis=0))
    turned = []
    for j in range(3 * channels):
        source, at = (spread, j) if j < 2 * channels else (spread_filt, j - 2 * channels)
        re = source[:rows, at * width : (at + 1) * width]
        im = source[rows:, at * width : (at + 1) * width]
        turned.append(jnp.concatenate([re * twist[0] - im * twist[1], re * twist[1] + im * twist[0]], axis=1))
    high, low = halves(jnp.concatenate(turned, axis=0))
    spectra = dot(high, second[0]) + dot(low, second[0]) + dot(high, second[1])

    def spectrum(j):
        block = spectra[j * rows : (j + 1) * rows]
        return block[:, :width], block[:, width:]

    products = []
    for c in range(channels):
        mr, mi = spectrum(2 * c)
        gr, gi = spectrum(2 * c + 1)
        hr, hi = spectrum(2 * channels + c)
        products.append(jnp.concatenate([mr * hr - mi * hi, mr * hi + mi * hr], axis=1))
        products.append(jnp.concatenate([gr * hr + gi * hi, gi * hr - gr * hi], axis=1))
        products.append(jnp.concatenate([gr * mr + gi * mi, gi * mr - gr * mi], axis=1))
    high, low = halves(jnp.concatenate(products, axis=0))
    back = dot(high, second_back[0]) + dot(low, second_back[0]) + dot(high, second_back[1])
    columns = []
    for j in range(3 * channels):
        re = back[j * rows : (j + 1) * rows, :width]
        im = back[j * rows : (j + 1) * rows, width:]
        columns.append(jnp.concatenate([re * twist[0] + im * twist[1], im * twist[0] - re * twist[1]], axis=0))
    high, low = halves(jnp.concatenate(columns, axis=1))
    result = dot(first_back, jnp.concatenate([high, high, low], axis=0))
    scale = 1.0 / math.sqrt(rows * width)
    sums = []
    for c in range(channels):
        convolved, mixed_grad, filter_grad = (
            result[:, (3 * c + j) * width : (3 * c + j + 1) * width] for j in range(3)
        )
        store(0, c, filtered[0, c] * convolved)
        inner = [grads[c] * convolved, mixed_grad * filtered[2, c], mixed_grad * filtered[1, c]]
        for i in range(3):
            g = inner[i]
            grad = taps(i, 0, c) * g + taps(i, 1, c) * sooner(g, 1, lane, row) + taps(i, 2, c) * sooner(g, 2, lane, row)
            store(1 + i, c, grad)
            for j in range(3):
                sums.append(((i, j, c), jnp.sum(g * shifted[i, c][j], axis=0, keepdims=True) * scale))
        store(4, c, filter_grad * scale)
    store_sums(sums)


MESH = pl.DeviceIdType.MESH
CORES = 2


def exchange_kernel(parts, channels, across, q_hbm, k_hbm, v_hbm, g_hbm, h_hbm, taps_hbm, first_hbm, twist_hbm, second_hbm, back_hbm, first_back_hbm,
                    got_ref, got_wide_ref, got_sums_ref,
                    raw, taps_ref, first_ref, twist_ref, second_ref, back_ref, first_back_ref, tap_rows, wide, wide_h, sum_rows,
                    send_a, send_h, recv_a, recv_h, send_out, send_wide, send_sums, line_sums, in_sems, send_sems, recv_sems):
    me = lax.axis_index("ctx")
    batch = channels // 2
    fields = 4 * batch
    others = parts - 1
    far = parts // (CORES * across)
    core, z, x = me % CORES, (me // CORES) % across, me // (CORES * across)
    plane = [((x + j) % far) * (CORES * across) + (core + k) % CORES for j in range(far) for k in range(CORES)]
    plane_index = x * CORES + core

    def each_peer(visit):
        def turn(step, carry):
            shift = across // 2 + (1 - 2 * (step % 2)) * ((step + 1) // 2)
            row = (z + shift) % across
            for base in reversed(plane):
                visit(base + row * CORES)
            return carry

        lax.fori_loop(0, across - 1, turn, 0)
        for base in reversed(plane[1:]):
            visit(base + z * CORES)

    def push(source, target, n, d):
        pltpu.make_async_remote_copy(source, target, send_sems.at[n], recv_sems.at[n], device_id={"ctx": d}, device_id_type=MESH).start()

    def keep(source, target, n):
        pltpu.make_async_copy(source, target, recv_sems.at[n]).start()

    def wait_bytes(ref, sem):
        pltpu.make_async_copy(ref, ref, sem).wait()

    barrier = pltpu.get_barrier_semaphore()
    each_peer(lambda d: pl.semaphore_signal(barrier, inc=1, device_id={"ctx": d}, device_id_type=MESH))
    loads = [pltpu.make_async_copy(ref, raw.at[a], in_sems.at[a]) for a, ref in enumerate((q_hbm, k_hbm, v_hbm, g_hbm, h_hbm))]
    pairs = ((taps_hbm, taps_ref), (first_hbm, first_ref), (twist_hbm, twist_ref), (second_hbm, second_ref), (back_hbm, back_ref), (first_back_hbm, first_back_ref))
    tables = [pltpu.make_async_copy(ref, held, in_sems.at[5 + n]) for n, (ref, held) in enumerate(pairs)]
    for copy in loads + tables:
        copy.start()

    for a in (4, 0, 1, 2, 3):
        loads[a].wait()
        columns = raw[a].astype(F32).T
        for c in range(channels):
            block = columns[c * parts : (c + 1) * parts]
            if a < 4:
                wide[c // batch, pl.ds(a * batch + c % batch, parts, stride=fields), :] = block
            else:
                wide_h[pl.ds(c, parts, stride=channels), :] = block
        if a == 4:
            for d in range(parts):
                send_h[d] = wide_h[d * channels : (d + 1) * channels, :].astype(BF16)
    for b in range(2):
        send_a[b] = wide[b].reshape(parts, fields, wide.shape[2]).astype(BF16)
    tables[0].wait()
    lane = lax.broadcasted_iota(jnp.int32, (3, taps_ref.shape[2]), 1)
    for i in range(3):
        taps_i = taps_ref[i].astype(F32)
        for c in range(channels):
            mine = jnp.sum(jnp.where(lane == me + c * parts, taps_i, 0.0), axis=1, keepdims=True)
            tap_rows[c, 3 * i : 3 * i + 3, :] = jnp.broadcast_to(mine, (3, tap_rows.shape[2]))

    pl.semaphore_wait(barrier, others)

    def send_first(d):
        push(send_h.at[d], recv_h.at[me], 0, d)
        push(send_a.at[0, d], recv_a.at[0, me], 1, d)

    each_peer(send_first)
    each_peer(lambda d: push(send_a.at[1, d], recv_a.at[1, me], 2, d))
    keep(send_h.at[me], recv_h.at[me], 0)
    for b in range(2):
        keep(send_a.at[b, me], recv_a.at[b, me], 1 + b)
    for copy in tables[1:]:
        copy.wait()
    sum_rows[...] = jnp.zeros_like(sum_rows)

    def run(b):
        if b == 0:
            wait_bytes(recv_h, recv_sems.at[0])
            for d in range(parts):
                wide_h[d * channels : (d + 1) * channels, :] = recv_h[d].astype(F32)
        wait_bytes(recv_a.at[b], recv_sems.at[1 + b])
        wide[b] = recv_a[b].astype(F32).reshape(parts * fields, wide.shape[2])

        def load(a, c):
            if a < 4:
                return wide[b, pl.ds(a * batch + c, parts, stride=fields), :]
            return wide_h[pl.ds(b * batch + c, parts, stride=channels), :]

        def taps(i, j, c):
            return tap_rows[b * batch + c, 3 * i + j : 3 * i + j + 1, :]

        def store(a, c, value):
            if a < 4:
                wide[b, pl.ds(a * batch + c, parts, stride=fields), :] = value
            else:
                wide_h[pl.ds(b * batch + c, parts, stride=channels), :] = value

        def store_sums(sums):
            for (i, j, c), value in sums:
                at = (i * 3 + j) * channels + b * batch + c
                sum_rows[at : at + 1, :] = value

        layer(load, taps, first_ref[...], twist_ref, second_ref, back_ref, first_back_ref[...], store, store_sums, batch)
        send_out[b] = wide[b].reshape(parts, fields, wide.shape[2]).astype(BF16)
        for d in range(parts):
            send_wide[b, d] = wide_h[d * channels + b * batch : d * channels + (b + 1) * batch, :]

    def send_back(b):
        def visit(d):
            push(send_out.at[b, d], got_ref.at[b, me], 3 + b, d)
            push(send_wide.at[b, d], got_wide_ref.at[b, me], 5 + b, d)

        each_peer(visit)
        keep(send_out.at[b, me], got_ref.at[b, me], 3 + b)
        keep(send_wide.at[b, me], got_wide_ref.at[b, me], 5 + b)

    run(0)
    send_back(0)
    run(1)
    high, low = halves(sum_rows[...])
    ones = jnp.ones((8, high.shape[1]), BF16)
    along = (((1,), (1,)), ((), ()))
    totals = lax.dot_general(ones, high, along, preferred_element_type=F32) + lax.dot_general(ones, low, along, preferred_element_type=F32)
    send_sums[...] = totals[0:1, :]
    for k in range(1, across):
        push(send_sums, line_sums.at[z], 7, plane[0] + ((z + k) % across) * CORES)
    keep(send_sums, line_sums.at[z], 7)
    send_back(1)
    wait_bytes(line_sums, recv_sems.at[7])
    for base in plane[1:]:
        push(line_sums, got_sums_ref.at[plane_index], 8, base + z * CORES)
    keep(line_sums, got_sums_ref.at[plane_index], 8)
    for n, ref in enumerate((recv_h, recv_a.at[0], recv_a.at[1], got_ref.at[0], got_ref.at[1], got_wide_ref.at[0], got_wide_ref.at[1], line_sums, got_sums_ref)):
        sent = ref.at[pl.ds(0, ref.shape[0] - 1)]
        wait_bytes(sent, send_sems.at[n])
    for n, ref in ((3, got_ref.at[0]), (4, got_ref.at[1]), (5, got_wide_ref.at[0]), (6, got_wide_ref.at[1]), (8, got_sums_ref)):
        wait_bytes(ref, recv_sems.at[n])


def finish_kernel(parts, channels, across, got_ref, got_wide_ref, got_sums_ref, out_hbm, q_hbm, k_hbm, v_hbm, h_hbm, taps_hbm,
                  wide, wide_h, sums, turned, done, done_h, done_taps, sems):
    batch = channels // 2
    fields = 4 * batch
    copies = []

    def put(source, target):
        copies.append(pltpu.make_async_copy(source, target, sems.at[len(copies)]))
        copies[-1].start()

    for d in range(parts):
        for b in range(2):
            wide_h[d * channels + b * batch : d * channels + (b + 1) * batch, :] = got_wide_ref[b, d]
        at = d // (CORES * across) * CORES + d % CORES
        sums[d : d + 1, :] = got_sums_ref[at, (d // CORES) % across]
    blocks = [wide_h[pl.ds(c, parts, stride=channels), :] for c in range(channels)]
    done_h[...] = jnp.concatenate(blocks, axis=0).T
    put(done_h, h_hbm)
    turned[...] = sums[...].T
    rows = jnp.concatenate([turned[pl.ds(c, 9, stride=channels), :] for c in range(channels)], axis=1)
    for i in range(3):
        done_taps[i] = rows[3 * i : 3 * i + 3]
    put(done_taps, taps_hbm)
    for b in range(2):
        wide[b] = got_ref[b].astype(F32).reshape(parts * fields, wide.shape[2])
    for a, ref in enumerate((out_hbm, q_hbm, k_hbm, v_hbm)):
        blocks = [wide[c // batch, pl.ds(a * batch + c % batch, parts, stride=fields), :] for c in range(channels)]
        done[a] = jnp.concatenate(blocks, axis=0).T.astype(BF16)
        put(done.at[a], ref)
    for copy in copies:
        copy.wait()


def local(query_in, key_in, value_in, long_filter, short_taps, out_grad):
    rows, width = query_in.shape
    parts = lax.axis_size("ctx")
    across = 8 if parts == 64 else parts // 4
    channels = width // parts
    fields = 2 * channels
    tables = [jnp.asarray(t) for t in transform_tables(parts, rows)]
    vmem = pl.BlockSpec(memory_space=pltpu.VMEM)
    hbm = pl.BlockSpec(memory_space=pl.ANY)
    planes = parts // across
    both = (2, parts, fields, rows)
    got = pl.pallas_call(
        lambda *refs: exchange_kernel(parts, channels, across, *refs),
        out_shape=(
            pltpu.VMEM(both, BF16),
            pltpu.VMEM((2, parts, 2, rows), F32),
            pltpu.VMEM((planes, across, 1, rows), F32),
        ),
        in_specs=[hbm] * 11,
        out_specs=(vmem, vmem, vmem),
        scratch_shapes=[pltpu.VMEM((5, rows, width), BF16), pltpu.VMEM(short_taps.shape, BF16)]
        + [pltpu.VMEM(t.shape, t.dtype) for t in tables]
        + [
            pltpu.VMEM((channels, 16, rows), F32),
            pltpu.VMEM((2, parts * fields, rows), F32),
            pltpu.VMEM((parts * channels, rows), F32),
            pltpu.VMEM((rows, rows), F32),
            pltpu.VMEM(both, BF16),
            pltpu.VMEM((parts, channels, rows), BF16),
            pltpu.VMEM(both, BF16),
            pltpu.VMEM((parts, channels, rows), BF16),
            pltpu.VMEM(both, BF16),
            pltpu.VMEM((2, parts, 2, rows), F32),
            pltpu.VMEM((1, rows), F32),
            pltpu.VMEM((across, 1, rows), F32),
            pltpu.SemaphoreType.DMA((11,)),
            pltpu.SemaphoreType.DMA((9,)),
            pltpu.SemaphoreType.DMA((9,)),
        ],
        compiler_params=pltpu.CompilerParams(collective_id=0, has_side_effects=True),
        name="exchange_and_layer",
    )(query_in, key_in, value_in, out_grad, long_filter, short_taps, *tables)
    got = [pltpu.with_memory_space_constraint(g, pltpu.VMEM) for g in got]
    field = jax.ShapeDtypeStruct((rows, width), BF16)
    return pl.pallas_call(
        lambda *refs: finish_kernel(parts, channels, across, *refs),
        out_shape=(field, field, field, field, jax.ShapeDtypeStruct((rows, width), F32), jax.ShapeDtypeStruct(short_taps.shape, F32)),
        in_specs=[vmem] * 3,
        out_specs=(hbm,) * 6,
        scratch_shapes=[
            pltpu.VMEM((2, parts * fields, rows), F32),
            pltpu.VMEM((parts * channels, rows), F32),
            pltpu.VMEM((parts, rows), F32),
            pltpu.VMEM((rows, parts), F32),
            pltpu.VMEM((4, rows, width), BF16),
            pltpu.VMEM((rows, width), F32),
            pltpu.VMEM(short_taps.shape, F32),
            pltpu.SemaphoreType.DMA((6,)),
        ],
        name="finish",
    )(*got)


def solution(mesh):
    placed = P("ctx", "tp")
    taps_placed = P(None, None, "tp")
    return jax.shard_map(
        local,
        mesh=mesh,
        in_specs=(placed, placed, placed, placed, taps_placed, placed),
        out_specs=(placed, placed, placed, placed, placed, taps_placed),
        check_vma=False,
    )
```
